32 devices in a mesh: parts: 2 (over y), off: 4 (over z), depth: 2 (over x), shot: 2 (over core).
Axes of the slice: x: 2, y: 2, z: 4, core: 2. Of those that a mesh axis runs over, the one named last changes fastest.
Arguments:
- image: bfloat16 [64, 32, 32, 256], P('off', None, 'depth'), may hold values from -4 to 4
- offset_of: int32 [64], P('off'), may hold values from 0 to 63, each once
- background: bfloat16 [4, 32, 32, 256], P(('parts', 'shot'), 'off', 'depth'), parts along dimension 0, may hold values from -6 to 6
- wave_now: float32 [4, 32, 32, 256], P(('parts', 'shot'), 'off', 'depth'), parts along dimension 0, may hold values from -6 to 6
- wave_prev: float32 [4, 32, 32, 256], P(('parts', 'shot'), 'off', 'depth'), parts along dimension 0, may hold values from -6 to 6
- courant: float32 [32, 32, 256], P('off', 'depth'), may hold values from 0.02 to 0.15
Outputs:
- wave_next: float32 [4, 32, 32, 256], P(('parts', 'shot'), 'off', 'depth'), parts along dimension 0
The draws below stay inside these ranges and needn't reach their ends.
There are 2 independent parts, one for each index of `parts`. The reference program is written for one: setup_inputs(seed, part) draws one part's arguments, and reference() takes and returns one part's arrays. A program takes and returns all parts, laid end to end along the dimension named above; an argument that names none is the same for every part. Nothing has to cross between parts.
Inputs may be any that keep to these rules, and one draw needn't show every extreme that they name: Each value appears once; image column k holds offset offset_of[k] - 32 cells along x.
All inputs are finite; a program needn't handle non-finite values.
Results may differ from the reference program's by a relative error of at most 0.0003.
Values may be sent and summed in bfloat16 or wider, within the bound.
A program may use at most 64 MiB of HBM per device.

```python
import math
import jax
import jax.numpy as jnp
from jax import lax

H = 64
NX = 256
NY = 32
NZ = 32
SHOTS = 2


def spiked(result, own_key, source, target, parts, factor):
    owner, partner = [(jnp.arange(result.shape[dim]) // (result.shape[dim] // parts)).reshape([-1 if axis == dim else 1 for axis in range(result.ndim)]) for dim in (source, target)]
    chosen = jax.random.permutation(own_key, parts)[partner]
    strong = (owner == chosen) | (owner == (partner + parts // 2) % parts)
    return jnp.where(strong, factor * result, result)


def block_levels(stream_key, shape, pieces, least, largest):
    def one(dim, parts):
        steps = jax.random.uniform(jax.random.fold_in(jax.random.fold_in(stream_key, 6), dim), (parts,), jnp.float32, least / len(pieces), largest / len(pieces))
        return jnp.repeat(jnp.exp(steps), shape[dim] // parts).reshape((-1,) + (1,) * (len(shape) - dim - 1))

    factor_of = one(*pieces[0])
    for cut in pieces[1:]:
        factor_of = factor_of * one(*cut)
    return factor_of


def normal_values(stream_key, extent, deviation, limit, cuts=(), dtype=jnp.bfloat16):
    level = block_levels(stream_key, extent, cuts, -0.22, 0.18) if cuts else 1.0
    entries = jax.random.normal(stream_key, extent, jnp.float32) * deviation * level
    return jnp.minimum(jnp.maximum(entries, -limit), limit).astype(dtype)


def heavy_noise(stream_key, shape, spread, reach, cuts, heavy, kind=jnp.bfloat16):
    values = spread * jax.random.normal(stream_key, shape, jnp.float32)
    if cuts:
        values = values * block_levels(stream_key, shape, cuts, -0.22, 0.18)
    return jnp.clip(spiked(values, jax.random.fold_in(stream_key, 3), *heavy), -reach, reach).astype(kind)


def setup_inputs(seed: int = 0, part: int = 0) -> dict:
    keys = jax.random.split(jax.random.key(seed), 7)
    part_keys = jax.random.split(jax.random.fold_in(keys[6], part), 7)
    return {
        "image": heavy_noise(keys[0], (H, NY, NZ, NX), 0.5, 4.0, ((0, 4), (2, 2)), (0, 1, 4, 2.0)),
        "offset_of": jax.random.permutation(keys[1], H).astype(jnp.int32),
        "background": normal_values(part_keys[2], (SHOTS, NY, NZ, NX), 1.0, 6.0, ((0, 2), (1, 4), (2, 2))),
        "wave_now": normal_values(part_keys[3], (SHOTS, NY, NZ, NX), 1.0, 6.0, ((0, 2), (1, 4), (2, 2)), jnp.float32),
        "wave_prev": normal_values(part_keys[4], (SHOTS, NY, NZ, NX), 1.0, 6.0, ((0, 2), (1, 4), (2, 2)), jnp.float32),
        "courant": jnp.clip(jnp.exp(math.log(0.15) - 2.014903 * jax.random.uniform(keys[5], (NY, NZ, NX), jnp.float32) ** block_levels(keys[5], (NY, NZ, NX), ((0, 4), (1, 2)), -0.2, 0.2)), 0.02, 0.15),
    }


STENCIL = (-205.0 / 72.0, 8.0 / 5.0, -1.0 / 5.0, 8.0 / 315.0, -1.0 / 560.0)


def laplace(padded, rows_y, rows_z, cols_x):
    extended = jnp.pad(padded, ((0, 0), (0, 0), (4, 4)))
    centre = extended[4:4 + rows_y, 4:4 + rows_z, 4:4 + cols_x]
    running = 3.0 * STENCIL[0] * centre
    for radius in range(1, 5):
        beside_all = extended[4 + radius:4 + radius + rows_y, 4:4 + rows_z, 4:4 + cols_x]
        beside_all = beside_all + extended[4 - radius:4 - radius + rows_y, 4:4 + rows_z, 4:4 + cols_x]
        beside_all = beside_all + extended[4:4 + rows_y, 4 + radius:4 + radius + rows_z, 4:4 + cols_x]
        beside_all = beside_all + extended[4:4 + rows_y, 4 - radius:4 - radius + rows_z, 4:4 + cols_x]
        beside_all = beside_all + extended[4:4 + rows_y, 4:4 + rows_z, 4 + radius:4 + radius + cols_x]
        beside_all = beside_all + extended[4:4 + rows_y, 4:4 + rows_z, 4 - radius:4 - radius + cols_x]
        running = running + STENCIL[radius] * beside_all
    return running


def reference(image, offset_of, background, wave_now, wave_prev, courant):
    half_span = H // 2

    def one_shot(inputs):
        backdrop, current, previous = inputs
        extended_bg = jnp.pad(backdrop, ((0, 0), (0, 0), (half_span, half_span)))

        def add_column(column, running):
            offset_cells = (offset_of[column] - half_span).astype(jnp.int32)
            image_col = lax.dynamic_index_in_dim(image, column, 0, keepdims=False)
            starts = (jnp.zeros((), jnp.int32), jnp.zeros((), jnp.int32), (half_span - offset_cells).astype(jnp.int32))
            shifted = lax.dynamic_slice(extended_bg, starts, (NY, NZ, NX))
            return running + image_col.astype(jnp.float32) * shifted.astype(jnp.float32)

        source = lax.fori_loop(0, H, add_column, jnp.zeros((NY, NZ, NX), jnp.float32))
        padded = jnp.pad(current, ((4, 4), (4, 4), (0, 0)))
        bending = laplace(padded, NY, NZ, NX)
        return 2.0 * current - previous + courant * (bending + source)

    return lax.map(one_shot, (background, wave_now, wave_prev))
```

```python
import functools

import jax
import jax.numpy as jnp
from jax import lax
from jax.experimental import pallas as pl
from jax.experimental.pallas import tpu as pltpu
from jax.sharding import PartitionSpec as P

H = 64
STENCIL = (-205.0 / 72.0, 8.0 / 5.0, -1.0 / 5.0, 8.0 / 315.0, -1.0 / 560.0)
R = 4
LANES = 128
TOP = 32767.0
PIECES = 4
MESH = pl.DeviceIdType.MESH


def kernel(
    n, nd,
    off_hbm, img_hbm, bg_hbm, now_hbm, prev_hbm, cour_hbm,
    out_ref,
    img, bg, wext, prev, cour, shift, acc, part_out, part_in, scale_out, scale_in,
    off_ref, load_sem, img_sem, bg_send, bg_recv, halo_send, halo_recv, p_send, p_recv, s_send, s_recv,
):
    K, _, Z, X = img.shape
    Y = out_ref.shape[1]
    me = lax.axis_index("off")
    dep = lax.axis_index("depth")
    has = {"l": me > 0, "r": me < n - 1, "u": dep > 0, "d": dep < nd - 1}
    near = {"l": {"off": me - 1}, "r": {"off": me + 1},
            "u": {"depth": dep - 1}, "d": {"depth": dep + 1}}

    fin = out_ref.at[0]

    own = wext.at[pl.ds(R, Y), pl.ds(8, Z), :]
    ld_bg = pltpu.make_async_copy(bg_hbm.at[0], bg.at[me], load_sem.at[0])
    ld_now = pltpu.make_async_copy(now_hbm.at[0], own, load_sem.at[1])
    ld_prev = pltpu.make_async_copy(prev_hbm.at[0], prev, load_sem.at[2])
    ld_cour = pltpu.make_async_copy(cour_hbm, cour, load_sem.at[3])
    ld_off = pltpu.make_async_copy(off_hbm, off_ref, load_sem.at[4])
    ld_off.start()
    ld_bg.start()
    ld_now.start()

    def img_load(j):
        rows = pl.ds(j * Y, Y)
        return pltpu.make_async_copy(img_hbm.at[:, rows], img.at[:, rows], img_sem.at[j])

    img_load(me).start()
    for t in range(1, n):
        @pl.when(me - t >= 0)
        def _():
            img_load(me - t).start()

        @pl.when(me + t < n)
        def _():
            img_load(me + t).start()
    ld_prev.start()
    ld_cour.start()

    barrier = pltpu.get_barrier_semaphore()
    for side in "lrud":
        @pl.when(has[side])
        def _():
            pl.semaphore_signal(barrier, inc=1, device_id=near[side], device_id_type=MESH)

    def clear(rows, cols):
        wext[rows, cols, :] = jnp.zeros((rows.size, cols.size, X), jnp.float32)

    edge = {"l": (pl.ds(0, R), pl.ds(8, Z)), "r": (pl.ds(R + Y, R), pl.ds(8, Z)),
            "u": (pl.ds(R, Y), pl.ds(0, 8)), "d": (pl.ds(R, Y), pl.ds(8 + Z, 8))}
    for side in "lrud":
        @pl.when(jnp.logical_not(has[side]))
        def _():
            clear(*edge[side])

    lead = lax.broadcasted_iota(jnp.int32, (X, X), 1) - lax.broadcasted_iota(jnp.int32, (X, X), 0)

    def build(k, carry):
        h = off_ref[k] - H // 2
        shift[k] = jnp.where(lead == h, 1.0, 0.0).astype(jnp.bfloat16)
        return carry

    ld_off.wait()
    lax.fori_loop(0, K, build, 0)
    ld_bg.wait()
    ld_now.wait()
    count = sum(has[s].astype(jnp.int32) for s in "lrud")
    pl.semaphore_wait(barrier, count)

    step = Y // PIECES if Y % PIECES == 0 else Y
    pieces = Y // step

    def bg_copy(j, c, target, slot):
        block = bg.at[j, pl.ds(c * step, step)]
        return pltpu.make_async_remote_copy(
            src_ref=block, dst_ref=block, send_sem=bg_send.at[slot, j * pieces + c],
            recv_sem=bg_recv.at[j * pieces + c], device_id={"off": target},
            device_id_type=MESH)

    mine = {"l": (pl.ds(R, R), pl.ds(8, Z)), "r": (pl.ds(Y, R), pl.ds(8, Z)),
            "u": (pl.ds(R, Y), pl.ds(8, 8)), "d": (pl.ds(R, Y), pl.ds(Z, 8))}
    other = {"l": "r", "r": "l", "u": "d", "d": "u"}
    num = {"l": 0, "r": 1, "u": 2, "d": 3}

    def halo_copy(side):
        there = other[side]
        return pltpu.make_async_remote_copy(
            src_ref=wext.at[mine[side][0], mine[side][1], :],
            dst_ref=wext.at[edge[there][0], edge[there][1], :],
            send_sem=halo_send.at[num[side]], recv_sem=halo_recv.at[num[there]],
            device_id=near[side], device_id_type=MESH)

    for c in range(pieces):
        for slot, side in enumerate("lr"):
            @pl.when(has[side])
            def _():
                bg_copy(me, c, near[side]["off"], slot).start()
    for side in "lrud":
        @pl.when(has[side])
        def _():
            halo_copy(side).start()


    group = 4 if K % 4 == 0 else 1

    lane1 = lax.broadcasted_iota(jnp.int32, (8, LANES), 1)

    def partial(j, dst, slot):
        def body(y, carry):
            for zt in range(Z // 8):
                src = bg[j, y, :, :].astype(jnp.float32)[zt * 8 : zt * 8 + 8]
                half = H // 2
                zero = jnp.zeros((8, LANES), jnp.float32)
                tiles = [pltpu.roll(src[:, x : x + LANES], half, 1) for x in range(0, X, LANES)]
                ext = []
                for q in range(X // LANES + 1):
                    lo = tiles[q - 1] if q > 0 else zero
                    hi = tiles[q] if q < X // LANES else zero
                    ext.append(jnp.where(lane1 < half, lo, hi))
                acc_t = [None] * (X // LANES)
                for k in range(K):
                    o = half - (off_ref[k] - half)
                    r = [pltpu.roll(t, LANES - o, 1) for t in ext]
                    keep = lane1 < LANES - o
                    im = img[k, j * Y + y].astype(jnp.float32)[zt * 8 : zt * 8 + 8]
                    for q in range(X // LANES):
                        moved = jnp.where(keep, r[q], r[q + 1])
                        term = im[:, q * LANES : q * LANES + LANES] * moved
                        acc_t[q] = term if acc_t[q] is None else acc_t[q] + term
                dst[slot, y, pl.ds(zt * 8, 8), :] = jnp.concatenate(acc_t, axis=1)
            return carry

        lax.fori_loop(0, Y, body, 0)

    def fold(full):
        top = jnp.max(full, axis=0)
        rows8 = functools.reduce(jnp.maximum, [top[z : z + 8] for z in range(0, Z, 8)])
        return functools.reduce(
            jnp.maximum, [rows8[:, x : x + LANES] for x in range(0, X, LANES)])

    def spread(small):
        return jnp.concatenate(
            [jnp.concatenate([small] * (X // LANES), axis=1)] * (Z // 8), axis=0)

    def encode(j):
        top = fold(jnp.abs(acc[1]))
        scale_out[j] = top * (1.0 / TOP)
        up = spread(jnp.where(top > 0.0, TOP / top, 0.0))
        for y in range(Y):
            whole = jnp.round(jnp.clip(acc[1, y] * up, -TOP, TOP)).astype(jnp.int32)
            part_out[j, y] = whole.astype(jnp.int16)

    def decoded(j):
        down = spread(scale_in[j])
        return part_in[j].astype(jnp.int32).astype(jnp.float32) * down[None]

    def part_copies(j, slot):
        return [
            pltpu.make_async_remote_copy(
                src_ref=src.at[j], dst_ref=dst.at[slot], send_sem=send.at[j],
                recv_sem=recv.at[slot], device_id={"off": j}, device_id_type=MESH)
            for src, dst, send, recv in (
                (scale_out, scale_in, s_send, s_recv), (part_out, part_in, p_send, p_recv))
        ]

    def arrivals(t):
        return ((me - t, me - t >= 0, 1), (me + t, me + t < n, -1))

    def onward(t, sign):
        if t % 2 == 0:
            return ()
        spots = [(me + hop * sign, slot) for slot, hop in ((1, 2), (0, 1))]
        return [(to, jnp.logical_and(to >= 0, to < n), slot) for to, slot in spots]

    img_load(me).wait()
    partial(me, acc, 0)

    def send_partial(j, ok):
        @pl.when(ok)
        def _():
            img_load(j).wait()
            partial(j, acc, 1)
            encode(j)
            for copy in part_copies(j, me):
                copy.start()

    order = [1] + [t for low in range(2, n, 2) for t in (low + 1, low) if t < n]
    for t in order:
        for c in range(pieces):
            for j, ok, sign in arrivals(t):
                @pl.when(ok)
                def _():
                    bg_copy(j, c, me, 0).wait_recv()
            for j, ok, sign in arrivals(t):
                for to, there, slot in onward(t, sign):
                    @pl.when(jnp.logical_and(ok, there))
                    def _():
                        bg_copy(j, c, to, slot).start()
        for j, ok, sign in arrivals(t):
            send_partial(j, ok)

    ld_prev.wait()
    ld_cour.wait()
    for side in "lrud":
        @pl.when(has[side])
        def _():
            halo_copy(side).wait_send()
            pltpu.make_async_remote_copy(
                src_ref=wext.at[mine[side][0], mine[side][1], :],
                dst_ref=wext.at[edge[side][0], edge[side][1], :],
                send_sem=halo_send.at[num[side]], recv_sem=halo_recv.at[num[side]],
                device_id=near[side], device_id_type=MESH).wait_recv()

    lane = lax.broadcasted_iota(jnp.int32, (Z, X), 1)

    def plane(y, carry):
        centre = wext[y + R, pl.ds(8, Z), :]
        running = 3.0 * STENCIL[0] * centre
        for r in range(1, R + 1):
            beside = wext[y + R + r, pl.ds(8, Z), :] + wext[y + R - r, pl.ds(8, Z), :]
            beside = beside + wext[y + R, pl.ds(8 + r, Z), :]
            beside = beside + wext[y + R, pl.ds(8 - r, Z), :]
            beside = beside + jnp.where(lane < X - r, pltpu.roll(centre, X - r, 1), 0.0)
            beside = beside + jnp.where(lane >= r, pltpu.roll(centre, r, 1), 0.0)
            running = running + STENCIL[r] * beside
        fin[y] = 2.0 * centre - prev[y] + cour[y] * (running + acc[0, y])
        return carry

    lax.fori_loop(0, Y, plane, 0)

    for t in range(1, n):
        for j, ok in ((me - t, me - t >= 0), (me + t, me + t < n)):
            @pl.when(ok)
            def _():
                for copy in part_copies(j, j):
                  copy.wait_recv()
                fin[...] = fin[...] + cour[...] * decoded(j)

    for c in range(pieces):
        for slot, side in enumerate("lr"):
            @pl.when(has[side])
            def _():
                bg_copy(me, c, near[side]["off"], slot).wait_send()
    for t in range(1, n):
        for j, ok, sign in arrivals(t):
            @pl.when(ok)
            def _():
                for copy in part_copies(j, me):
                    copy.wait_send()
            for to, there, slot in onward(t, sign):
                @pl.when(jnp.logical_and(ok, there))
                def _():
                    for c in range(pieces):
                        bg_copy(j, c, to, slot).wait_send()


def on_device(n, nd, image, offset_of, background, wave_now, wave_prev, courant):
    K, rows, Z, X = image.shape
    Y = wave_now.shape[1]
    f32 = jnp.float32
    anywhere = pl.BlockSpec(memory_space=pltpu.HBM)
    dma = pltpu.SemaphoreType.DMA
    return pl.pallas_call(
        functools.partial(kernel, n, nd),
        out_shape=jax.ShapeDtypeStruct(wave_now.shape, f32),
        in_specs=[anywhere] * 6,
        out_specs=pl.BlockSpec(memory_space=pltpu.VMEM),
        scratch_shapes=[
            pltpu.VMEM((K, rows, Z, X), jnp.bfloat16),
            pltpu.VMEM((n, Y, Z, X), jnp.bfloat16),
            pltpu.VMEM((Y + 2 * R, Z + 16, X), f32),
            pltpu.VMEM((Y, Z, X), f32),
            pltpu.VMEM((Y, Z, X), f32),
            pltpu.VMEM((K, X, X), jnp.bfloat16),
            pltpu.VMEM((2, Y, Z, X), f32),
            pltpu.VMEM((n, Y, Z, X), jnp.int16),
            pltpu.VMEM((n, Y, Z, X), jnp.int16),
            pltpu.VMEM((n, 8, LANES), f32),
            pltpu.VMEM((n, 8, LANES), f32),
            pltpu.SMEM((K,), jnp.int32), dma((5,)), dma((n,)), dma((2, n * PIECES)), dma((n * PIECES,)), dma((4,)), dma((4,)),
            dma((n,)), dma((n,)), dma((n,)), dma((n,)),
        ],
        compiler_params=pltpu.CompilerParams(
            collective_id=0, has_side_effects=True, vmem_limit_bytes=50331648),
        name="born_step",
    )(*[pltpu.with_memory_space_constraint(a, pltpu.HBM) for a in
        (offset_of, image, background, wave_now, wave_prev, courant)])


def solution(mesh):
    wave = P(("parts", "shot"), "off", "depth", None)
    return jax.shard_map(
        functools.partial(on_device, mesh.shape["off"], mesh.shape["depth"]),
        mesh=mesh,
        in_specs=(
            P("off", None, "depth", None),
            P("off"),
            wave,
            wave,
            wave,
            P("off", "depth", None),
        ),
        out_specs=wave,
        check_vma=False,
    )
```

```python
import functools

import jax
import jax.numpy as jnp
from jax import lax
from jax.experimental import pallas as pl
from jax.experimental.pallas import tpu as pltpu
from jax.sharding import PartitionSpec as P

STENCIL = (-205.0 / 72.0, 8.0 / 5.0, -1.0 / 5.0, 8.0 / 315.0, -1.0 / 560.0)
R = 4
LANES = 128
TOP = 32767.0
PIECES = 2
MESH = pl.DeviceIdType.MESH


def kernel(
    n, nd,
    off_hbm, img_hbm, bg_hbm, now_hbm, prev_hbm, cour_hbm,
    out_ref,
    off_ref, img, raw, bg, wext, prev, cour, shift, acc,
    part_out, part_in, scale_out, scale_in, tally,
    edge_out, edge_in, edge_scale_out, edge_scale_in, edge_tally,
    load_sem, img_sem, ready, near_ready, bg_recv, bg_send, fwd_send,
    halo_send, halo_recv, p_recv, p_send,
):
    K, _, Z, X = img.shape
    Y = out_ref.shape[1]
    step = part_out.shape[2]
    pieces = part_out.shape[1]
    half = K * n // 2
    me = lax.axis_index("off")
    dep = lax.axis_index("depth")
    other_shot = lax.axis_size("shot") - 1 - lax.axis_index("shot")
    has = {"l": me > 0, "r": me < n - 1, "u": dep > 0, "d": dep < nd - 1}
    near = {"l": {"off": me - 1}, "r": {"off": me + 1},
            "u": {"depth": dep - 1}, "d": {"depth": dep + 1}}
    fin = out_ref.at[0]

    def far(j):
        return {"off": j, "shot": other_shot}

    ld_bg = pltpu.make_async_copy(bg_hbm.at[0], raw, load_sem.at[0])
    ld_off = pltpu.make_async_copy(off_hbm, off_ref, load_sem.at[1])
    ld_now = pltpu.make_async_copy(
        now_hbm.at[0], wext.at[pl.ds(R, Y), pl.ds(8, Z), :], load_sem.at[2])
    ld_prev = pltpu.make_async_copy(prev_hbm.at[0], prev, load_sem.at[3])
    ld_cour = pltpu.make_async_copy(cour_hbm, cour, load_sem.at[4])
    ld_bg.start()
    ld_off.start()
    ld_now.start()

    barrier = pltpu.get_barrier_semaphore()
    for t in range(1, n):
        @pl.when(me + t < n)
        def _():
            pl.semaphore_signal(barrier, inc=1, device_id=far(me + t), device_id_type=MESH)
    for side in "rd":
        @pl.when(has[side])
        def _():
            pl.semaphore_signal(barrier, inc=1, device_id=near[side], device_id_type=MESH)

    def img_load(j):
        rows = pl.ds(j * Y, Y)
        return pltpu.make_async_copy(img_hbm.at[:, rows], img.at[:, rows], img_sem.at[j])

    def order(i):
        last = me == n - 1
        rest = jnp.where(jnp.logical_or(i - 1 < me, last), i - 1, i + 1)
        first = jnp.where(last, me - 1, me + 1)
        high = jnp.where(i == 0, first, jnp.where(i == 1, 0, rest))
        low = jnp.where(jnp.logical_and(i == 0, me == 1), 0, i + 1)
        return jnp.where(me < 2, low, high)

    img_load(me).start()

    @pl.loop(0, n - 1)
    def _(i):
        img_load(order(i)).start()

    ld_prev.start()
    ld_cour.start()

    def clear(rows, cols):
        wext[rows, cols, :] = jnp.zeros((rows.size, cols.size, X), jnp.float32)

    edge = {"l": (pl.ds(0, R), pl.ds(8, Z)), "r": (pl.ds(R + Y, R), pl.ds(8, Z)),
            "u": (pl.ds(R, Y), pl.ds(0, 8)), "d": (pl.ds(R, Y), pl.ds(8 + Z, 8))}
    for side in "lrud":
        @pl.when(jnp.logical_not(has[side]))
        def _():
            clear(*edge[side])

    mine = {"l": pl.ds(R, R), "r": pl.ds(Y, R), "u": pl.ds(0, 8), "d": pl.ds(Z - 8, 8)}
    other = {"l": "r", "r": "l", "u": "d", "d": "u"}
    num = {"l": 0, "r": 1, "u": 2, "d": 3}

    def halo_copies(side):
        there = other[side]
        if side in "ud":
            pairs = [(now_hbm.at[0, :, mine[side], :], wext.at[edge[there][0], edge[there][1], :])]
        else:
            pairs = [(edge_out.at[num[side]], edge_in.at[num[there]]),
                     (edge_scale_out.at[num[side]], edge_scale_in.at[num[there]])]
        return [
            pltpu.make_async_remote_copy(
                src_ref=src, dst_ref=dst, send_sem=halo_send.at[num[side]],
                recv_sem=halo_recv.at[num[there]], device_id=near[side], device_id_type=MESH)
            for src, dst in pairs
        ]

    def halo_wait(side, sem):
        if side in "ud":
            there = wext.at[edge[side][0], edge[side][1], :]
            pltpu.make_async_copy(there, there, sem.at[num[side]]).wait()
        else:
            pltpu.make_async_copy(edge_tally, edge_tally, sem.at[num[side]]).wait()

    lower = me + has["l"].astype(jnp.int32) + has["u"].astype(jnp.int32)

    @pl.when(lower > 0)
    def _():
        pl.semaphore_wait(barrier, lower)
    for t in range(n - 1, 0, -1):
        @pl.when(me - t >= 0)
        def _():
            pl.semaphore_signal(ready.at[me], inc=1, device_id=far(me - t), device_id_type=MESH)
    for side, slot in (("l", 0), ("u", 1)):
        @pl.when(has[side])
        def _():
            pl.semaphore_signal(near_ready.at[slot], inc=1, device_id=near[side], device_id_type=MESH)

    @pl.when(has["u"])
    def _():
        for copy in halo_copies("u"):
            copy.start()

    tiles = X // LANES

    def encode(total, whole_ref, scale_ref, *at):
        top = jnp.max(jnp.abs(total), axis=(0, 1))[None]
        top = functools.reduce(
            jnp.maximum, [top[:, q * LANES : (q + 1) * LANES] for q in range(tiles)])
        scale_ref[at] = top * (1.0 / TOP)
        up = jnp.concatenate([jnp.where(top > 0.0, TOP / top, 0.0)] * tiles, axis=1)
        whole = jnp.round(jnp.clip(total * up[None], -TOP, TOP)).astype(jnp.int32)
        whole_ref[at] = whole.astype(jnp.int16)

    def decode(whole_ref, scale_ref, *at):
        down = jnp.concatenate([scale_ref[at]] * tiles, axis=1)
        return whole_ref[at].astype(jnp.int32).astype(jnp.float32) * down[None]

    ld_bg.wait()
    for y in range(Y):
        bg[me, y] = pltpu.roll(raw[y].astype(jnp.float32), half, 1).astype(jnp.bfloat16)

    def piece_of(j, c):
        return bg.at[j, pl.ds(c * step, step)]

    def bg_copy(j, c, target, send):
        return pltpu.make_async_remote_copy(
            src_ref=piece_of(j, c), dst_ref=piece_of(j, c), send_sem=send,
            recv_sem=bg_recv.at[j * pieces + c], device_id=target, device_id_type=MESH)

    def bg_sent(j, target, send):
        return pltpu.make_async_remote_copy(
            src_ref=bg.at[j], dst_ref=bg.at[j], send_sem=send,
            recv_sem=bg_recv.at[j * pieces], device_id=target, device_id_type=MESH)

    def relayed(j, g):
        return jnp.logical_and(j >= 1, g >= j + 2)

    def direct(g):
        ok = jnp.logical_and(g >= 0, g < n)
        return jnp.logical_and(ok, jnp.logical_not(relayed(me, g)))

    def send_own(g):
        for c in range(pieces):
            bg_copy(me, c, far(g), bg_send.at[g]).start()

    for t in range(1, n):
        @pl.when(direct(me - t))
        def _():
            send_own(me - t)

    ld_now.wait()
    for side in "lr":
        encode(wext[mine[side], pl.ds(8, Z), :], edge_out, edge_scale_out, num[side])

    @pl.when(has["l"])
    def _():
        for copy in halo_copies("l"):
            copy.start()

    lead = lax.broadcasted_iota(jnp.int32, (2 * LANES, LANES), 0) - lax.broadcasted_iota(
        jnp.int32, (2 * LANES, LANES), 1)
    ld_off.wait()
    for k in range(K):
        move = 2 * half - off_ref[k]
        shift[k // 2, :, pl.ds(k % 2 * LANES, LANES)] = jnp.where(
            lead == move, 1.0, 0.0).astype(jnp.bfloat16)

    lane = lax.broadcasted_iota(jnp.int32, (step * Z, LANES), 1)

    def partial(j, c):
        rows = bg[j, pl.ds(c * step, step)].reshape(step * Z, X)
        cols = [rows[:, q * LANES : (q + 1) * LANES] for q in range(tiles)]
        zero = jnp.zeros_like(cols[0])
        cols.append(jnp.where(lane < half, cols[0], zero))
        cols[0] = jnp.where(lane < half, zero, cols[0])
        lhs = jnp.concatenate(
            [jnp.concatenate([cols[q], cols[q + 1]], axis=1) for q in range(tiles)], axis=0)
        total = None
        for k in range(K):
            if k % 2 == 0:
                moved = jnp.dot(lhs, shift[k // 2], preferred_element_type=jnp.float32)
            side = moved[:, k % 2 * LANES : (k % 2 + 1) * LANES]
            line = jnp.concatenate(
                [side[q * step * Z : (q + 1) * step * Z] for q in range(tiles)], axis=1)
            term = img[k, pl.ds(j * Y + c * step, step)].astype(jnp.float32) * line.reshape(step, Z, X)
            total = term if total is None else total + term
        return total

    def part_send(j, c):
        for s, (src, dst) in enumerate(((part_out, part_in), (scale_out, scale_in))):
            pltpu.make_async_remote_copy(
                src_ref=src.at[j, c], dst_ref=dst.at[me, c], send_sem=p_send.at[s],
                recv_sem=p_recv.at[me], device_id=far(j), device_id_type=MESH).start()

    img_load(me).wait()
    for c in range(pieces):
        acc[pl.ds(c * step, step)] = partial(me, c)

    for t in range(1, n):
        @pl.when(direct(me + t))
        def _():
            pl.semaphore_wait(ready.at[me + t], 1)
            send_own(me + t)
    @pl.when(has["d"])
    def _():
        pl.semaphore_wait(near_ready.at[1], 1)
        for copy in halo_copies("d"):
            copy.start()

    @pl.when(has["r"])
    def _():
        pl.semaphore_wait(near_ready.at[0], 1)
        for copy in halo_copies("r"):
            copy.start()

    @pl.loop(0, n - 1)
    def _(i):
        j = order(i)

        onward = jnp.where(j < me, me + 1, me - 1)
        go_on = jnp.logical_and(
            jnp.logical_and(onward >= 0, onward < n), relayed(j, onward))
        for c in range(pieces):
            bg_copy(j, c, far(j), bg_send.at[j]).wait_recv()

            @pl.when(go_on)
            def _():
                bg_copy(j, c, {"off": onward}, fwd_send.at[j]).start()

            if c == 0:
                img_load(j).wait()

                @pl.when(jnp.logical_and(j > me, relayed(me, j)))
                def _():
                    pl.semaphore_wait(ready.at[j], 1)
            encode(partial(j, c), part_out, scale_out, j, c)
            part_send(j, c)

    ld_prev.wait()
    ld_cour.wait()
    for side in "lrud":
      @pl.when(has[side])
      def _():
          halo_wait(side, halo_recv)
          if side in "lr":
              wext[edge[side][0], edge[side][1], :] = decode(edge_in, edge_scale_in, num[side])

    wide = lax.broadcasted_iota(jnp.int32, (Z, X), 1)

    def plane(y, carry):
        centre = wext[y + R, pl.ds(8, Z), :]
        running = 3.0 * STENCIL[0] * centre
        for r in range(1, R + 1):
            beside = wext[y + R + r, pl.ds(8, Z), :] + wext[y + R - r, pl.ds(8, Z), :]
            beside = beside + wext[y + R, pl.ds(8 + r, Z), :]
            beside = beside + wext[y + R, pl.ds(8 - r, Z), :]
            beside = beside + jnp.where(wide < X - r, pltpu.roll(centre, X - r, 1), 0.0)
            beside = beside + jnp.where(wide >= r, pltpu.roll(centre, r, 1), 0.0)
            running = running + STENCIL[r] * beside
        fin[y] = 2.0 * centre - prev[y] + cour[y] * (running + acc[y])
        return carry

    lax.fori_loop(0, Y, plane, 0)

    @pl.loop(0, n - 1)
    def _(i):
        j = order(i)

        pltpu.make_async_copy(tally, tally, p_recv.at[j]).wait()
        for c in range(pieces):
            rows = pl.ds(c * step, step)
            fin[rows] = fin[rows] + cour[rows] * decode(part_in, scale_in, j, c)

    for side in "lrud":
      @pl.when(has[side])
      def _():
          halo_wait(side, halo_send)
    for t in range(1, n):
      for g in (me - t, me + t):
          @pl.when(direct(g))
          def _():
              bg_sent(me, far(g), bg_send.at[g]).wait_send()

    @pl.loop(0, n - 1)
    def _(i):
      j = order(i)
      onward = jnp.where(j < me, me + 1, me - 1)
      go_on = jnp.logical_and(
          jnp.logical_and(onward >= 0, onward < n), relayed(j, onward))

      @pl.when(go_on)
      def _():
          bg_sent(j, {"off": onward}, fwd_send.at[j]).wait_send()

    for s, src in enumerate((part_out, scale_out)):
      sent = src.at[pl.ds(0, n - 1)]
      pltpu.make_async_copy(sent, sent, p_send.at[s]).wait()


def on_device(n, nd, image, offset_of, background, wave_now, wave_prev, courant):
    K, rows, Z, X = image.shape
    Y = wave_now.shape[1]
    f32 = jnp.float32
    pieces = PIECES if Y % PIECES == 0 else 1
    step = Y // pieces
    lines = (Y * Z * X * 2) // (LANES * 4) + pieces
    dma = pltpu.SemaphoreType.DMA
    regular = pltpu.SemaphoreType.REGULAR
    return pl.pallas_call(
        functools.partial(kernel, n, nd),
        out_shape=jax.ShapeDtypeStruct(wave_now.shape, f32),
        in_specs=[pl.BlockSpec(memory_space=pltpu.HBM)] * 6,
        out_specs=pl.BlockSpec(memory_space=pltpu.VMEM),
        scratch_shapes=[
            pltpu.SMEM((K,), jnp.int32),
            pltpu.VMEM((K, rows, Z, X), jnp.bfloat16),
            pltpu.VMEM((Y, Z, X), jnp.bfloat16),
            pltpu.VMEM((n, Y, Z, X), jnp.bfloat16),
            pltpu.VMEM((Y + 2 * R, Z + 16, X), f32),
            pltpu.VMEM((Y, Z, X), f32),
            pltpu.VMEM((Y, Z, X), f32),
            pltpu.VMEM(((K + 1) // 2, 2 * LANES, 2 * LANES), jnp.bfloat16),
            pltpu.VMEM((Y, Z, X), f32),
            pltpu.VMEM((n, pieces, step, Z, X), jnp.int16),
            pltpu.VMEM((n, pieces, step, Z, X), jnp.int16),
            pltpu.VMEM((n, pieces, 1, LANES), f32),
            pltpu.VMEM((n, pieces, 1, LANES), f32),
            pltpu.VMEM((lines, LANES), f32),
            pltpu.VMEM((2, R, Z, X), jnp.int16),
            pltpu.VMEM((2, R, Z, X), jnp.int16),
            pltpu.VMEM((2, 1, LANES), f32),
            pltpu.VMEM((2, 1, LANES), f32),
            pltpu.VMEM(((R * Z * X * 2) // (LANES * 4) + 1, LANES), f32),
            dma((5,)), dma((n,)), regular((n,)), regular((2,)),
            dma((n * pieces,)), dma((n,)), dma((n,)),
            dma((4,)), dma((4,)), dma((n,)), dma((2,)),
        ],
        compiler_params=pltpu.CompilerParams(
            collective_id=0, has_side_effects=True, vmem_limit_bytes=50331648),
        name="born_step",
    )(*[pltpu.with_memory_space_constraint(a, pltpu.HBM) for a in
        (offset_of, image, background, wave_now, wave_prev, courant)])


def solution(mesh):
    wave = P(("parts", "shot"), "off", "depth", None)
    return jax.shard_map(
        functools.partial(on_device, mesh.shape["off"], mesh.shape["depth"]),
        mesh=mesh,
        in_specs=(
            P("off", None, "depth", None),
            P("off"),
            wave,
            wave,
            wave,
            P("off", "depth", None),
        ),
        out_specs=wave,
        check_vma=False,
    )
```

```python
import functools

import jax
import jax.numpy as jnp
from jax import lax
from jax.experimental import pallas as pl
from jax.experimental.pallas import tpu as pltpu
from jax.sharding import PartitionSpec as P

STENCIL = (-205.0 / 72.0, 8.0 / 5.0, -1.0 / 5.0, 8.0 / 315.0, -1.0 / 560.0)
R = 4
LANES = 128
TOP = 32767.0
PIECES = 2
MESH = pl.DeviceIdType.MESH


def kernel(
    n, nd,
    off_hbm, img_hbm, bg_hbm, now_hbm, prev_hbm, cour_hbm,
    out_ref,
    off_ref, img, raw, bg, wext, local, shift, acc,
    part_out, part_in, scale_out, scale_in, pend, join_in, join_scale, tally,
    edge_out, edge_in, edge_scale_out, edge_scale_in, edge_tally, piece_tally,
    load_sem, img_sem, ready, near_ready, bg_recv, bg_send,
    halo_send, halo_recv, p_recv, join_recv, p_send,
):
    K, _, Z, X = img.shape
    Y = out_ref.shape[1]
    step = part_out.shape[2]
    pieces = part_out.shape[1]
    half = K * n // 2
    me = lax.axis_index("off")
    dep = lax.axis_index("depth")
    other_shot = lax.axis_size("shot") - 1 - lax.axis_index("shot")
    has = {"l": me > 0, "r": me < n - 1, "u": dep > 0, "d": dep < nd - 1}
    near = {"l": {"off": me - 1}, "r": {"off": me + 1},
            "u": {"depth": dep - 1}, "d": {"depth": dep + 1}}
    fin = out_ref.at[0]

    def far(j):
        return {"off": j, "shot": other_shot}

    ld_bg = pltpu.make_async_copy(bg_hbm.at[0], raw, load_sem.at[0])
    ld_off = pltpu.make_async_copy(off_hbm, off_ref, load_sem.at[1])
    ld_now = pltpu.make_async_copy(
        now_hbm.at[0], wext.at[pl.ds(R, Y), pl.ds(8, Z), :], load_sem.at[2])
    prev, cour = local.at[0], local.at[1]
    ld_prev = pltpu.make_async_copy(prev_hbm.at[0], prev, load_sem.at[3])
    ld_cour = pltpu.make_async_copy(cour_hbm, cour, load_sem.at[3])
    ld_local = pltpu.make_async_copy(local, local, load_sem.at[3])
    ld_bg.start()
    ld_off.start()
    ld_now.start()

    barrier = pltpu.get_barrier_semaphore()
    for t in range(1, n):
        @pl.when(me + t < n)
        def _():
            pl.semaphore_signal(barrier, inc=1, device_id=far(me + t), device_id_type=MESH)
    for side in "rd":
        @pl.when(has[side])
        def _():
            pl.semaphore_signal(barrier, inc=1, device_id=near[side], device_id_type=MESH)

    def img_load(j):
        rows = pl.ds(j * Y, Y)
        sem = img_sem.at[jnp.where(j == me, 0, 1)]
        return pltpu.make_async_copy(img_hbm.at[:, rows], img.at[:, rows], sem)

    def order(i):
        mid = jnp.where(i == 0, 0, jnp.where(i == 1, n - 1, i))
        rest = jnp.where(i < me, i - 1, i + 1)
        last = me == n - 1
        first = jnp.where(last, me - 1, 0)
        second = jnp.where(last, 0, me - 1)
        high = jnp.where(i == 0, first, jnp.where(i == 1, second, rest))
        low = jnp.where(i == 0, 2, jnp.where(i == 1, 1, i + 1))
        return jnp.where(me == 0, low, jnp.where(me == 1, mid, high))

    img_load(me).start()

    @pl.loop(0, n - 1)
    def _(i):
        img_load(order(i)).start()

    ld_prev.start()
    ld_cour.start()

    def clear(rows, cols):
        wext[rows, cols, :] = jnp.zeros((rows.size, cols.size, X), jnp.float32)

    edge = {"l": (pl.ds(0, R), pl.ds(8, Z)), "r": (pl.ds(R + Y, R), pl.ds(8, Z)),
            "u": (pl.ds(R, Y), pl.ds(0, 8)), "d": (pl.ds(R, Y), pl.ds(8 + Z, 8))}
    for side in "lrud":
        @pl.when(jnp.logical_not(has[side]))
        def _():
            clear(*edge[side])

    mine = {"l": pl.ds(R, R), "r": pl.ds(Y, R), "u": pl.ds(0, 8), "d": pl.ds(Z - 8, 8)}
    other = {"l": "r", "r": "l", "u": "d", "d": "u"}
    num = {"l": 0, "r": 1, "u": 2, "d": 3}

    def halo_copies(side):
        there = other[side]
        if side in "ud":
            pairs = [(now_hbm.at[0, :, mine[side], :], wext.at[edge[there][0], edge[there][1], :])]
        else:
            pairs = [(edge_out.at[num[side]], edge_in.at[num[there]]),
                     (edge_scale_out.at[num[side]], edge_scale_in.at[num[there]])]
        return [
            pltpu.make_async_remote_copy(
                src_ref=src, dst_ref=dst, send_sem=halo_send.at[num[side] // 2],
                recv_sem=halo_recv.at[num[side] // 2], device_id=near[side], device_id_type=MESH)
            for src, dst in pairs
        ]

    def halo_wait(sem):
        for axis, (low, high) in enumerate(("lr", "ud")):
            count = has[low].astype(jnp.int32) + has[high].astype(jnp.int32)
            for c in (1, 2):
                whole = (edge_tally.at[pl.ds(0, c)], wext.at[pl.ds(R, Y), pl.ds(0, 8 * c), :])[axis]

                @pl.when(count == c)
                def _():
                    pltpu.make_async_copy(whole, whole, sem.at[axis]).wait()

    lower = me + has["l"].astype(jnp.int32) + has["u"].astype(jnp.int32)

    @pl.when(lower > 0)
    def _():
        pl.semaphore_wait(barrier, lower)
    for t in range(n - 1, 0, -1):
        @pl.when(me - t >= 0)
        def _():
            pl.semaphore_signal(ready.at[me - 1], inc=1, device_id=far(me - t), device_id_type=MESH)
    for side in "lu":
        @pl.when(has[side])
        def _():
            pl.semaphore_signal(near_ready.at[0], inc=1, device_id=near[side], device_id_type=MESH)

    @pl.when(has["u"])
    def _():
        for copy in halo_copies("u"):
            copy.start()

    tiles = X // LANES

    def encode(total, whole_ref, scale_ref, *at):
        top = jnp.max(jnp.abs(total), axis=(0, 1))[None]
        top = functools.reduce(
            jnp.maximum, [top[:, q * LANES : (q + 1) * LANES] for q in range(tiles)])
        scale_ref[at] = top * (1.0 / TOP)
        up = jnp.concatenate([jnp.where(top > 0.0, TOP / top, 0.0)] * tiles, axis=1)
        whole = jnp.round(jnp.clip(total * up[None], -TOP, TOP)).astype(jnp.int32)
        whole_ref[at] = whole.astype(jnp.int16)

    def decode(whole_ref, scale_ref, *at):
        down = jnp.concatenate([scale_ref[at]] * tiles, axis=1)
        return whole_ref[at].astype(jnp.int32).astype(jnp.float32) * down[None]

    ld_bg.wait()
    for y in range(Y):
        bg[me, y] = pltpu.roll(raw[y].astype(jnp.float32), half, 1).astype(jnp.bfloat16)

    def piece_of(j, c):
        return bg.at[j, pl.ds(c * step, step)]

    def place(j, g):
        return j - (j > g).astype(jnp.int32)

    def bg_copy(j, c, target, slot, send):
        return pltpu.make_async_remote_copy(
            src_ref=piece_of(j, c), dst_ref=piece_of(j, c), send_sem=send,
            recv_sem=bg_recv.at[slot * pieces + c], device_id=target, device_id_type=MESH)

    def bg_sent(sem, count, most):
        for c in range(1, most):
            whole = bg.at[pl.ds(0, c)]

            @pl.when(count == c)
            def _():
                pltpu.make_async_copy(whole, whole, sem).wait()

    def relayed(j, g):
        left = jnp.logical_and(g == 0, j >= 3)
        right = jnp.logical_and(g >= j + 2, j >= 1)
        return jnp.where(g < j, left, right)

    def relay(j):
        onward = jnp.where(j < me, me + 1, me - 1)
        ok = jnp.logical_and(onward >= 0, onward < n)
        return onward, jnp.logical_and(ok, relayed(j, onward))

    def direct(g):
        ok = jnp.logical_and(g >= 0, g < n)
        return jnp.logical_and(ok, jnp.logical_not(relayed(me, g)))

    def send_own(g):
        for c in range(pieces):
            bg_copy(me, c, far(g), place(me, g), bg_send.at[0]).start()

    for t in range(n - 1, 0, -1):
        @pl.when(direct(me - t))
        def _():
            send_own(me - t)

    ld_now.wait()
    for side in "lr":
        encode(wext[mine[side], pl.ds(8, Z), :], edge_out, edge_scale_out, num[side])

    @pl.when(has["l"])
    def _():
        for copy in halo_copies("l"):
            copy.start()

    lead = lax.broadcasted_iota(jnp.int32, (2 * LANES, LANES), 0) - lax.broadcasted_iota(
        jnp.int32, (2 * LANES, LANES), 1)
    ld_off.wait()
    for k in range(K):
        move = 2 * half - off_ref[k]
        shift[k // 2, :, pl.ds(k % 2 * LANES, LANES)] = jnp.where(
            lead == move, 1.0, 0.0).astype(jnp.bfloat16)

    lane = lax.broadcasted_iota(jnp.int32, (step * Z, LANES), 1)

    def partial(j, c):
        rows = bg[j, pl.ds(c * step, step)].reshape(step * Z, X)
        cols = [rows[:, q * LANES : (q + 1) * LANES] for q in range(tiles)]
        zero = jnp.zeros_like(cols[0])
        cols.append(jnp.where(lane < half, cols[0], zero))
        cols[0] = jnp.where(lane < half, zero, cols[0])
        lhs = jnp.concatenate(
            [jnp.concatenate([cols[q], cols[q + 1]], axis=1) for q in range(tiles)], axis=0)
        total = None
        for k in range(K):
            if k % 2 == 0:
                moved = jnp.dot(lhs, shift[k // 2], preferred_element_type=jnp.float32)
            side = moved[:, k % 2 * LANES : (k % 2 + 1) * LANES]
            line = jnp.concatenate(
                [side[q * step * Z : (q + 1) * step * Z] for q in range(tiles)], axis=1)
            term = img[k, pl.ds(j * Y + c * step, step)].astype(jnp.float32) * line.reshape(step, Z, X)
            total = term if total is None else total + term
        return total

    joins = jnp.logical_and(me >= 1, me < n - 1)

    def part_send(j, c):
        def copies(dsts, recv, target):
            for src, dst in zip((part_out, scale_out), dsts):
                pltpu.make_async_remote_copy(
                    src_ref=src.at[j, c], dst_ref=dst, send_sem=p_send.at[0],
                    recv_sem=recv, device_id=target, device_id_type=MESH).start()

        @pl.when(j == me + 2)
        def _():
            copies((join_in.at[c], join_scale.at[c]), join_recv.at[c], {"off": me + 1})

        @pl.when(j != me + 2)
        def _():
            copies((part_in.at[me, c], scale_in.at[me, c]), p_recv.at[place(me, j)], far(j))

    img_load(me).wait()
    for c in range(pieces):
        acc[pl.ds(c * step, step)] = partial(me, c)

    for t in range(1, n):
        @pl.when(direct(me + t))
        def _():
            pl.semaphore_wait(ready.at[me + t - 1], 1)
            send_own(me + t)

    higher = has["r"].astype(jnp.int32) + has["d"].astype(jnp.int32)

    @pl.when(higher > 0)
    def _():
        pl.semaphore_wait(near_ready.at[0], higher)
    for side in "rd":
        @pl.when(has[side])
        def _():
            for copy in halo_copies(side):
                copy.start()

    rest = img.at[:, pl.ds(0, (n - 1) * Y)]
    pltpu.make_async_copy(rest, rest, img_sem.at[1]).wait()

    @pl.loop(0, n - 1)
    def _(i):
        j = order(i)

        onward, go_on = relay(j)
        for c in range(pieces):
            bg_copy(j, c, far(j), place(j, me), bg_send.at[0]).wait_recv()

            @pl.when(go_on)
            def _():
                bg_copy(j, c, {"off": onward}, place(j, onward), bg_send.at[1]).start()

            if c == 0:
                @pl.when(jnp.logical_and(j > me, relayed(me, j)))
                def _():
                    pl.semaphore_wait(ready.at[j - 1], 1)
            total = partial(j, c)
            later = jnp.logical_and(joins, j == me + 1)

            @pl.when(later)
            def _():
                pend[pl.ds(c * step, step)] = total

            @pl.when(jnp.logical_not(later))
            def _():
                encode(total, part_out, scale_out, j, c)
                part_send(j, c)

    @pl.when(joins)
    def _():
        for c in range(pieces):
            pltpu.make_async_copy(piece_tally, piece_tally, join_recv.at[c]).wait()
            total = pend[pl.ds(c * step, step)] + decode(join_in, join_scale, c)
            encode(total, part_out, scale_out, me + 1, c)
            part_send(me + 1, c)

    ld_local.wait()
    halo_wait(halo_recv)
    for side in "lr":
        @pl.when(has[side])
        def _():
            wext[edge[side][0], edge[side][1], :] = decode(edge_in, edge_scale_in, num[side])

    wide = lax.broadcasted_iota(jnp.int32, (Z, X), 1)

    def plane(y, carry):
        centre = wext[y + R, pl.ds(8, Z), :]
        running = 3.0 * STENCIL[0] * centre
        for r in range(1, R + 1):
            beside = wext[y + R + r, pl.ds(8, Z), :] + wext[y + R - r, pl.ds(8, Z), :]
            beside = beside + wext[y + R, pl.ds(8 + r, Z), :]
            beside = beside + wext[y + R, pl.ds(8 - r, Z), :]
            beside = beside + jnp.where(wide < X - r, pltpu.roll(centre, X - r, 1), 0.0)
            beside = beside + jnp.where(wide >= r, pltpu.roll(centre, r, 1), 0.0)
            running = running + STENCIL[r] * beside
        fin[y] = 2.0 * centre - prev[y] + cour[y] * (running + acc[y])
        return carry

    lax.fori_loop(0, Y, plane, 0)

    @pl.loop(0, n - 1)
    def _(i):
        j = order(i)


        @pl.when(j != me - 2)
        def _():
            pltpu.make_async_copy(tally.at[0], tally.at[0], p_recv.at[place(j, me)]).wait()
            for c in range(pieces):
                rows = pl.ds(c * step, step)
                fin[rows] = fin[rows] + cour[rows] * decode(part_in, scale_in, j, c)

    halo_wait(halo_send)
    sent, passed = 0, 0
    for g in range(n):
      there = g != me
      sent = sent + jnp.logical_and(there, direct(g)).astype(jnp.int32)
      passed = passed + jnp.logical_and(there, relay(g)[1]).astype(jnp.int32)
    bg_sent(bg_send.at[0], sent, n)
    bg_sent(bg_send.at[1], passed, n - 1)
    pltpu.make_async_copy(tally, tally, p_send.at[0]).wait()


def on_device(n, nd, image, offset_of, background, wave_now, wave_prev, courant):
    K, rows, Z, X = image.shape
    Y = wave_now.shape[1]
    f32 = jnp.float32
    pieces = PIECES if Y % PIECES == 0 else 1
    step = Y // pieces
    lines = (Y * Z * X * 2) // (LANES * 4) + pieces
    dma = pltpu.SemaphoreType.DMA
    regular = pltpu.SemaphoreType.REGULAR
    return pl.pallas_call(
        functools.partial(kernel, n, nd),
        out_shape=jax.ShapeDtypeStruct(wave_now.shape, f32),
        in_specs=[pl.BlockSpec(memory_space=pltpu.HBM)] * 6,
        out_specs=pl.BlockSpec(memory_space=pltpu.VMEM),
        scratch_shapes=[
            pltpu.SMEM((K,), jnp.int32),
            pltpu.VMEM((K, rows, Z, X), jnp.bfloat16),
            pltpu.VMEM((Y, Z, X), jnp.bfloat16),
            pltpu.VMEM((n, Y, Z, X), jnp.bfloat16),
            pltpu.VMEM((Y + 2 * R, Z + 16, X), f32),
            pltpu.VMEM((2, Y, Z, X), f32),
            pltpu.VMEM(((K + 1) // 2, 2 * LANES, 2 * LANES), jnp.bfloat16),
            pltpu.VMEM((Y, Z, X), f32),
            pltpu.VMEM((n, pieces, step, Z, X), jnp.int16),
            pltpu.VMEM((n, pieces, step, Z, X), jnp.int16),
            pltpu.VMEM((n, pieces, 1, LANES), f32),
            pltpu.VMEM((n, pieces, 1, LANES), f32),
            pltpu.VMEM((Y, Z, X), f32),
            pltpu.VMEM((pieces, step, Z, X), jnp.int16),
            pltpu.VMEM((pieces, 1, LANES), f32),
            pltpu.VMEM((n - 1, lines, LANES), f32),
            pltpu.VMEM((2, R, Z, X), jnp.int16),
            pltpu.VMEM((2, R, Z, X), jnp.int16),
            pltpu.VMEM((2, 1, LANES), f32),
            pltpu.VMEM((2, 1, LANES), f32),
            pltpu.VMEM((2, (R * Z * X * 2) // (LANES * 4) + 1, LANES), f32),
            pltpu.VMEM((lines // pieces, LANES), f32),
            dma((4,)), dma((2,)), regular((n - 1,)), regular((1,)),
            dma(((n - 1) * pieces,)), dma((2,)), dma((2,)), dma((2,)),
            dma((n - 1,)), dma((pieces,)), dma((1,)),
        ],
        compiler_params=pltpu.CompilerParams(
            collective_id=0, has_side_effects=True, vmem_limit_bytes=50331648),
        name="born_step",
    )(*[pltpu.with_memory_space_constraint(a, pltpu.HBM) for a in
        (offset_of, image, background, wave_now, wave_prev, courant)])


def solution(mesh):
    wave = P(("parts", "shot"), "off", "depth", None)
    return jax.shard_map(
        functools.partial(on_device, mesh.shape["off"], mesh.shape["depth"]),
        mesh=mesh,
        in_specs=(
            P("off", None, "depth", None),
            P("off"),
            wave,
            wave,
            wave,
            P("off", "depth", None),
        ),
        out_specs=wave,
        check_vma=False,
    )
```

```python
import functools

import jax
import jax.numpy as jnp
from jax import lax
from jax.experimental import pallas as pl
from jax.experimental.pallas import tpu as pltpu
from jax.sharding import PartitionSpec as P

STENCIL = (-205.0 / 72.0, 8.0 / 5.0, -1.0 / 5.0, 8.0 / 315.0, -1.0 / 560.0)
R = 4
LANES = 128
TOP = 32767.0
PIECES = 2
MESH = pl.DeviceIdType.MESH


def kernel(
    n, nd,
    off_hbm, img_hbm, bg_hbm, now_hbm, prev_hbm, cour_hbm,
    out_ref,
    off_ref, img, raw, bg, wext, local, shift, acc,
    part_out, part_in, scale_out, scale_in, pend, join_in, join_scale, tally,
    edge_out, edge_in, edge_scale_out, edge_scale_in, edge_tally, piece_tally,
    load_sem, img_sem, ready, near_ready, bg_recv, bg_send,
    halo_send, halo_recv, p_recv, join_recv, p_send,
):
    K, _, Z, X = img.shape
    Y = out_ref.shape[1]
    step = part_out.shape[2]
    pieces = part_out.shape[1]
    half = K * n // 2
    me = lax.axis_index("off")
    dep = lax.axis_index("depth")
    shot = lax.axis_index("shot")
    other_shot = lax.axis_size("shot") - 1 - shot
    has = {"l": me > 0, "r": me < n - 1, "u": dep > 0, "d": dep < nd - 1}
    near = {"l": {"off": me - 1}, "r": {"off": me + 1},
            "u": {"depth": dep - 1}, "d": {"depth": dep + 1}}
    fin = out_ref.at[0]

    def far(j):
        return {"off": j, "shot": other_shot}

    ld_bg = pltpu.make_async_copy(bg_hbm.at[0], raw, load_sem.at[0])
    ld_off = pltpu.make_async_copy(off_hbm, off_ref, load_sem.at[1])
    ld_now = pltpu.make_async_copy(
        now_hbm.at[0], wext.at[pl.ds(R, Y), pl.ds(8, Z), :], load_sem.at[2])
    prev, cour = local.at[0], local.at[1]
    ld_prev = pltpu.make_async_copy(prev_hbm.at[0], prev, load_sem.at[3])
    ld_cour = pltpu.make_async_copy(cour_hbm, cour, load_sem.at[3])
    ld_local = pltpu.make_async_copy(local, local, load_sem.at[3])
    ld_bg.start()
    ld_off.start()
    ld_now.start()

    barrier = pltpu.get_barrier_semaphore()
    for t in range(1, n):
        @pl.when(me + t < n)
        def _():
            pl.semaphore_signal(barrier, inc=1, device_id=far(me + t), device_id_type=MESH)
    for side in "rd":
        @pl.when(has[side])
        def _():
            pl.semaphore_signal(barrier, inc=1, device_id=near[side], device_id_type=MESH)

    def img_load(j):
        rows = pl.ds(j * Y, Y)
        sem = img_sem.at[jnp.where(j == me, 0, 1)]
        return pltpu.make_async_copy(img_hbm.at[:, rows], img.at[:, rows], sem)

    def order(i):
        mid = jnp.where(i == 0, 0, jnp.where(i == 1, n - 1, i))
        rest = jnp.where(i < me, i - 1, i + 1)
        last = me == n - 1
        first = jnp.where(last, me - 1, 0)
        second = jnp.where(last, 0, me - 1)
        high = jnp.where(i == 0, first, jnp.where(i == 1, second, rest))
        low = jnp.where(i == 0, 2, jnp.where(i == 1, 1, i + 1))
        return jnp.where(me == 0, low, jnp.where(me == 1, mid, high))

    img_load(me).start()

    @pl.loop(0, n - 1)
    def _(i):
        img_load(order(i)).start()

    ld_prev.start()
    ld_cour.start()

    def clear(rows, cols):
        wext[rows, cols, :] = jnp.zeros((rows.size, cols.size, X), jnp.float32)

    edge = {"l": (pl.ds(0, R), pl.ds(8, Z)), "r": (pl.ds(R + Y, R), pl.ds(8, Z)),
            "u": (pl.ds(R, Y), pl.ds(0, 8)), "d": (pl.ds(R, Y), pl.ds(8 + Z, 8))}
    for side in "lrud":
        @pl.when(jnp.logical_not(has[side]))
        def _():
            clear(*edge[side])

    mine = {"l": pl.ds(R, R), "r": pl.ds(Y, R), "u": pl.ds(0, 8), "d": pl.ds(Z - 8, 8)}
    other = {"l": "r", "r": "l", "u": "d", "d": "u"}
    num = {"l": 0, "r": 1, "u": 2, "d": 3}

    def halo_copies(side):
        there = other[side]
        if side in "ud":
            pairs = [(now_hbm.at[0, :, mine[side], :], wext.at[edge[there][0], edge[there][1], :])]
        else:
            pairs = [(edge_out.at[num[side]], edge_in.at[num[there]]),
                     (edge_scale_out.at[num[side]], edge_scale_in.at[num[there]])]
        return [
            pltpu.make_async_remote_copy(
                src_ref=src, dst_ref=dst, send_sem=halo_send.at[num[side] // 2],
                recv_sem=halo_recv.at[num[side] // 2], device_id=near[side], device_id_type=MESH)
            for src, dst in pairs
        ]

    def halo_wait(sem):
        for axis, (low, high) in enumerate(("lr", "ud")):
            count = has[low].astype(jnp.int32) + has[high].astype(jnp.int32)
            for c in (1, 2):
                whole = (edge_tally.at[pl.ds(0, c)], wext.at[pl.ds(R, Y), pl.ds(0, 8 * c), :])[axis]

                @pl.when(count == c)
                def _():
                    pltpu.make_async_copy(whole, whole, sem.at[axis]).wait()

    lower = me + has["l"].astype(jnp.int32) + has["u"].astype(jnp.int32)

    @pl.when(lower > 0)
    def _():
        pl.semaphore_wait(barrier, lower)
    for t in range(n - 1, 0, -1):
        @pl.when(me - t >= 0)
        def _():
            pl.semaphore_signal(ready.at[me - 1], inc=1, device_id=far(me - t), device_id_type=MESH)
    for side in "lu":
        @pl.when(has[side])
        def _():
            pl.semaphore_signal(near_ready.at[0], inc=1, device_id=near[side], device_id_type=MESH)

    @pl.when(has["u"])
    def _():
        for copy in halo_copies("u"):
            copy.start()

    tiles = X // LANES

    def encode(total, whole_ref, scale_ref, *at):
        top = jnp.max(jnp.abs(total), axis=(0, 1))[None]
        top = functools.reduce(
            jnp.maximum, [top[:, q * LANES : (q + 1) * LANES] for q in range(tiles)])
        scale_ref[at] = top * (1.0 / TOP)
        up = jnp.concatenate([jnp.where(top > 0.0, TOP / top, 0.0)] * tiles, axis=1)
        whole = jnp.round(jnp.clip(total * up[None], -TOP, TOP)).astype(jnp.int32)
        whole_ref[at] = whole.astype(jnp.int16)

    def decode(whole_ref, scale_ref, *at):
        down = jnp.concatenate([scale_ref[at]] * tiles, axis=1)
        return whole_ref[at].astype(jnp.int32).astype(jnp.float32) * down[None]

    ld_bg.wait()
    for y in range(Y):
        bg[me, y] = pltpu.roll(raw[y].astype(jnp.float32), half, 1).astype(jnp.bfloat16)

    def piece_of(j, c):
        return bg.at[j, pl.ds(c * step, step)]

    def place(j, g):
        return j - (j > g).astype(jnp.int32)

    def bg_copy(j, c, target, slot, send):
        return pltpu.make_async_remote_copy(
            src_ref=piece_of(j, c), dst_ref=piece_of(j, c), send_sem=send,
            recv_sem=bg_recv.at[slot * pieces + c], device_id=target, device_id_type=MESH)

    def bg_sent(sem, count, most):
        for c in range(1, most):
            whole = bg.at[pl.ds(0, c)]

            @pl.when(count == c)
            def _():
                pltpu.make_async_copy(whole, whole, sem).wait()

    def relayed(j, g, core):
        left = jnp.logical_and(g == 0, j >= 3)
        right = jnp.logical_and(g >= j + 2, j >= 1)
        return jnp.where(g < j, left, right)

    def relay(j):
        onward = jnp.where(j < me, me + 1, me - 1)
        ok = jnp.logical_and(onward >= 0, onward < n)
        return onward, jnp.logical_and(ok, relayed(j, onward, other_shot))

    def direct(g):
        ok = jnp.logical_and(g >= 0, g < n)
        return jnp.logical_and(ok, jnp.logical_not(relayed(me, g, shot)))

    def send_own(g):
        for c in range(pieces):
            bg_copy(me, c, far(g), place(me, g), bg_send.at[0]).start()

    for t in range(n - 1, 0, -1):
        @pl.when(direct(me - t))
        def _():
            send_own(me - t)

    ld_now.wait()
    for side in "lr":
        encode(wext[mine[side], pl.ds(8, Z), :], edge_out, edge_scale_out, num[side])

    @pl.when(has["l"])
    def _():
        for copy in halo_copies("l"):
            copy.start()

    lead = lax.broadcasted_iota(jnp.int32, (2 * LANES, LANES), 0) - lax.broadcasted_iota(
        jnp.int32, (2 * LANES, LANES), 1)
    ld_off.wait()
    for k in range(K):
        move = 2 * half - off_ref[k]
        shift[k // 2, :, pl.ds(k % 2 * LANES, LANES)] = jnp.where(
            lead == move, 1.0, 0.0).astype(jnp.bfloat16)

    lane = lax.broadcasted_iota(jnp.int32, (step * Z, LANES), 1)

    def partial(j, c):
        rows = bg[j, pl.ds(c * step, step)].reshape(step * Z, X)
        cols = [rows[:, q * LANES : (q + 1) * LANES] for q in range(tiles)]
        zero = jnp.zeros_like(cols[0])
        cols.append(jnp.where(lane < half, cols[0], zero))
        cols[0] = jnp.where(lane < half, zero, cols[0])
        lhs = jnp.concatenate(
            [jnp.concatenate([cols[q], cols[q + 1]], axis=1) for q in range(tiles)], axis=0)
        total = None
        for k in range(K):
            if k % 2 == 0:
                moved = jnp.dot(lhs, shift[k // 2], preferred_element_type=jnp.float32)
            side = moved[:, k % 2 * LANES : (k % 2 + 1) * LANES]
            line = jnp.concatenate(
                [side[q * step * Z : (q + 1) * step * Z] for q in range(tiles)], axis=1)
            term = img[k, pl.ds(j * Y + c * step, step)].astype(jnp.float32) * line.reshape(step, Z, X)
            total = term if total is None else total + term
        return total

    joins = jnp.logical_and(me >= 1, me < n - 1)

    def part_send(j, c):
        def copies(dsts, recv, target):
            for src, dst in zip((part_out, scale_out), dsts):
                pltpu.make_async_remote_copy(
                    src_ref=src.at[j, c], dst_ref=dst, send_sem=p_send.at[0],
                    recv_sem=recv, device_id=target, device_id_type=MESH).start()

        @pl.when(j == me + 2)
        def _():
            copies((join_in.at[c], join_scale.at[c]), join_recv.at[c], {"off": me + 1})

        @pl.when(j != me + 2)
        def _():
            copies((part_in.at[me, c], scale_in.at[me, c]), p_recv.at[place(me, j)], far(j))

    img_load(me).wait()
    for c in range(pieces):
        acc[pl.ds(c * step, step)] = partial(me, c)

    for t in range(1, n):
        @pl.when(direct(me + t))
        def _():
            pl.semaphore_wait(ready.at[me + t - 1], 1)
            send_own(me + t)

    higher = has["r"].astype(jnp.int32) + has["d"].astype(jnp.int32)

    @pl.when(higher > 0)
    def _():
        pl.semaphore_wait(near_ready.at[0], higher)
    for side in "rd":
        @pl.when(has[side])
        def _():
            for copy in halo_copies(side):
                copy.start()

    rest = img.at[:, pl.ds(0, (n - 1) * Y)]
    pltpu.make_async_copy(rest, rest, img_sem.at[1]).wait()

    def laplace():
        ld_local.wait()
        halo_wait(halo_recv)
        for side in "lr":
            @pl.when(has[side])
            def _():
                wext[edge[side][0], edge[side][1], :] = decode(edge_in, edge_scale_in, num[side])

        wide = lax.broadcasted_iota(jnp.int32, (Z, X), 1)

        def plane(y, carry):
            centre = wext[y + R, pl.ds(8, Z), :]
            running = 3.0 * STENCIL[0] * centre
            for r in range(1, R + 1):
                beside = wext[y + R + r, pl.ds(8, Z), :] + wext[y + R - r, pl.ds(8, Z), :]
                beside = beside + wext[y + R, pl.ds(8 + r, Z), :]
                beside = beside + wext[y + R, pl.ds(8 - r, Z), :]
                beside = beside + jnp.where(wide < X - r, pltpu.roll(centre, X - r, 1), 0.0)
                beside = beside + jnp.where(wide >= r, pltpu.roll(centre, r, 1), 0.0)
                running = running + STENCIL[r] * beside
            fin[y] = 2.0 * centre - prev[y] + cour[y] * (running + acc[y])
            return carry

        lax.fori_loop(0, Y, plane, 0)

    early = jnp.logical_and(me >= 2, me < n - 1)

    @pl.loop(0, (n - 1) * pieces)
    def _(q):
        swap = jnp.where(q == 0, pieces, jnp.where(q <= pieces, q - 1, q))
        turns = jnp.where(q == 1, 2, jnp.where(q == 2, 1, q)) if pieces == 2 and n > 2 else q
        q = jnp.where(early, swap, jnp.where(me == 1, turns, q))
        i, c = q // pieces, q % pieces
        j = order(i)

        @pl.when(jnp.logical_and(me == 0, q == (n - 2) * pieces))
        def _():
            laplace()

        onward, go_on = relay(j)
        bg_copy(j, c, far(j), place(j, me), bg_send.at[0]).wait_recv()

        @pl.when(go_on)
        def _():
            bg_copy(j, c, {"off": onward}, place(j, onward), bg_send.at[1]).start()

        @pl.when(jnp.logical_and(c == 0, jnp.logical_and(j > me, relayed(me, j, shot))))
        def _():
            pl.semaphore_wait(ready.at[j - 1], 1)
        total = partial(j, c)
        later = jnp.logical_and(joins, j == me + 1)

        @pl.when(later)
        def _():
            pend[pl.ds(c * step, step)] = total

        @pl.when(jnp.logical_not(later))
        def _():
            encode(total, part_out, scale_out, j, c)
            part_send(j, c)

    @pl.when(joins)
    def _():
        for c in range(pieces):
            pltpu.make_async_copy(piece_tally, piece_tally, join_recv.at[c]).wait()
            total = pend[pl.ds(c * step, step)] + decode(join_in, join_scale, c)
            encode(total, part_out, scale_out, me + 1, c)
            part_send(me + 1, c)

    @pl.when(me > 0)
    def _():
        laplace()

    def drain():
        halo_wait(halo_send)
        sent, passed = 0, 0
        for g in range(n):
          there = g != me
          sent = sent + jnp.logical_and(there, direct(g)).astype(jnp.int32)
          passed = passed + jnp.logical_and(there, relay(g)[1]).astype(jnp.int32)
        bg_sent(bg_send.at[0], sent, n)
        bg_sent(bg_send.at[1], passed, n - 1)
        pltpu.make_async_copy(tally, tally, p_send.at[0]).wait()

    @pl.loop(0, n - 1)
    def _(i):
        j = order(i)

        @pl.when(i == n - 2)
        def _():
            drain()

        @pl.when(j != me - 2)
        def _():
            pltpu.make_async_copy(tally.at[0], tally.at[0], p_recv.at[place(j, me)]).wait()
            for c in range(pieces):
                rows = pl.ds(c * step, step)
                fin[rows] = fin[rows] + cour[rows] * decode(part_in, scale_in, j, c)


def on_device(n, nd, image, offset_of, background, wave_now, wave_prev, courant):
    K, rows, Z, X = image.shape
    Y = wave_now.shape[1]
    f32 = jnp.float32
    pieces = PIECES if Y % PIECES == 0 else 1
    step = Y // pieces
    lines = (Y * Z * X * 2) // (LANES * 4) + pieces
    dma = pltpu.SemaphoreType.DMA
    regular = pltpu.SemaphoreType.REGULAR
    return pl.pallas_call(
        functools.partial(kernel, n, nd),
        out_shape=jax.ShapeDtypeStruct(wave_now.shape, f32),
        in_specs=[pl.BlockSpec(memory_space=pltpu.HBM)] * 6,
        out_specs=pl.BlockSpec(memory_space=pltpu.VMEM),
        scratch_shapes=[
            pltpu.SMEM((K,), jnp.int32),
            pltpu.VMEM((K, rows, Z, X), jnp.bfloat16),
            pltpu.VMEM((Y, Z, X), jnp.bfloat16),
            pltpu.VMEM((n, Y, Z, X), jnp.bfloat16),
            pltpu.VMEM((Y + 2 * R, Z + 16, X), f32),
            pltpu.VMEM((2, Y, Z, X), f32),
            pltpu.VMEM(((K + 1) // 2, 2 * LANES, 2 * LANES), jnp.bfloat16),
            pltpu.VMEM((Y, Z, X), f32),
            pltpu.VMEM((n, pieces, step, Z, X), jnp.int16),
            pltpu.VMEM((n, pieces, step, Z, X), jnp.int16),
            pltpu.VMEM((n, pieces, 1, LANES), f32),
            pltpu.VMEM((n, pieces, 1, LANES), f32),
            pltpu.VMEM((Y, Z, X), f32),
            pltpu.VMEM((pieces, step, Z, X), jnp.int16),
            pltpu.VMEM((pieces, 1, LANES), f32),
            pltpu.VMEM((n - 1, lines, LANES), f32),
            pltpu.VMEM((2, R, Z, X), jnp.int16),
            pltpu.VMEM((2, R, Z, X), jnp.int16),
            pltpu.VMEM((2, 1, LANES), f32),
            pltpu.VMEM((2, 1, LANES), f32),
            pltpu.VMEM((2, (R * Z * X * 2) // (LANES * 4) + 1, LANES), f32),
            pltpu.VMEM((lines // pieces, LANES), f32),
            dma((4,)), dma((2,)), regular((n - 1,)), regular((1,)),
            dma(((n - 1) * pieces,)), dma((2,)), dma((2,)), dma((2,)),
            dma((n - 1,)), dma((pieces,)), dma((1,)),
        ],
        compiler_params=pltpu.CompilerParams(
            collective_id=0, has_side_effects=True, vmem_limit_bytes=50331648),
        name="born_step",
    )(*[pltpu.with_memory_space_constraint(a, pltpu.HBM) for a in
        (offset_of, image, background, wave_now, wave_prev, courant)])


def solution(mesh):
    wave = P(("parts", "shot"), "off", "depth", None)
    return jax.shard_map(
        functools.partial(on_device, mesh.shape["off"], mesh.shape["depth"]),
        mesh=mesh,
        in_specs=(
            P("off", None, "depth", None),
            P("off"),
            wave,
            wave,
            wave,
            P("off", "depth", None),
        ),
        out_specs=wave,
        check_vma=False,
    )
```

```python
import functools

import jax
import jax.numpy as jnp
from jax import lax
from jax.experimental import pallas as pl
from jax.experimental.pallas import tpu as pltpu
from jax.sharding import PartitionSpec as P

STENCIL = (-205.0 / 72.0, 8.0 / 5.0, -1.0 / 5.0, 8.0 / 315.0, -1.0 / 560.0)
R = 4
LANES = 128
TOP = 32767.0
PIECES = 2
MESH = pl.DeviceIdType.MESH


def kernel(
    n, nd,
    off_hbm, img_hbm, bg_hbm, now_hbm, prev_hbm, cour_hbm,
    out_ref,
    off_ref, img, raw, bg, wext, local, shift, acc,
    part_out, part_in, scale_out, scale_in, pend, join_in, join_scale, tally,
    edge_out, edge_in, edge_scale_out, edge_scale_in, edge_tally, piece_tally,
    load_sem, img_sem, ready, near_ready, bg_recv, bg_send,
    halo_send, halo_recv, p_recv, join_recv, p_send,
):
    K, _, Z, X = img.shape
    Y = out_ref.shape[1]
    step = part_out.shape[2]
    pieces = part_out.shape[1]
    half = K * n // 2
    me = lax.axis_index("off")
    dep = lax.axis_index("depth")
    shot = lax.axis_index("shot")
    other_shot = lax.axis_size("shot") - 1 - shot
    has = {"l": me > 0, "r": me < n - 1, "u": dep > 0, "d": dep < nd - 1}
    near = {"l": {"off": me - 1}, "r": {"off": me + 1},
            "u": {"depth": dep - 1}, "d": {"depth": dep + 1}}
    fin = out_ref.at[0]

    def far(j):
        return {"off": j, "shot": other_shot}

    ld_bg = pltpu.make_async_copy(bg_hbm.at[0], raw, load_sem.at[0])
    ld_off = pltpu.make_async_copy(off_hbm, off_ref, load_sem.at[1])
    ld_now = pltpu.make_async_copy(
        now_hbm.at[0], wext.at[pl.ds(R, Y), pl.ds(8, Z), :], load_sem.at[2])
    prev, cour = local.at[0], local.at[1]
    ld_prev = pltpu.make_async_copy(prev_hbm.at[0], prev, load_sem.at[3])
    ld_cour = pltpu.make_async_copy(cour_hbm, cour, load_sem.at[3])
    ld_local = pltpu.make_async_copy(local, local, load_sem.at[3])
    ld_bg.start()
    ld_off.start()
    ld_now.start()

    barrier = pltpu.get_barrier_semaphore()
    for t in range(1, n):
        @pl.when(me + t < n)
        def _():
            pl.semaphore_signal(barrier, inc=1, device_id=far(me + t), device_id_type=MESH)
    for side in "rd":
        @pl.when(has[side])
        def _():
            pl.semaphore_signal(barrier, inc=1, device_id=near[side], device_id_type=MESH)

    def img_load(j):
        rows = pl.ds(j * Y, Y)
        sem = img_sem.at[jnp.where(j == me, 0, 1)]
        return pltpu.make_async_copy(img_hbm.at[:, rows], img.at[:, rows], sem)

    def order(i):
        mid = jnp.where(i == 0, 0, jnp.where(i == 1, n - 1, i))
        rest = jnp.where(i < me, i - 1, i + 1)
        last = me == n - 1
        first = jnp.where(last, me - 1, 0)
        second = jnp.where(last, 0, me - 1)
        high = jnp.where(i == 0, first, jnp.where(i == 1, second, rest))
        low = jnp.where(i == 0, 2, jnp.where(i == 1, 1, i + 1))
        return jnp.where(me == 0, low, jnp.where(me == 1, mid, high))

    img_load(me).start()

    @pl.loop(0, n - 1)
    def _(i):
        img_load(order(i)).start()

    ld_prev.start()
    ld_cour.start()

    def clear(rows, cols):
        wext[rows, cols, :] = jnp.zeros((rows.size, cols.size, X), jnp.float32)

    edge = {"l": (pl.ds(0, R), pl.ds(8, Z)), "r": (pl.ds(R + Y, R), pl.ds(8, Z)),
            "u": (pl.ds(R, Y), pl.ds(0, 8)), "d": (pl.ds(R, Y), pl.ds(8 + Z, 8))}
    for side in "lrud":
        @pl.when(jnp.logical_not(has[side]))
        def _():
            clear(*edge[side])

    mine = {"l": pl.ds(R, R), "r": pl.ds(Y, R), "u": pl.ds(0, 8), "d": pl.ds(Z - 8, 8)}
    other = {"l": "r", "r": "l", "u": "d", "d": "u"}
    num = {"l": 0, "r": 1, "u": 2, "d": 3}

    def halo_copies(side):
        there = other[side]
        if side in "ud":
            pairs = [(now_hbm.at[0, :, mine[side], :], wext.at[edge[there][0], edge[there][1], :])]
        else:
            pairs = [(edge_out.at[num[side]], edge_in.at[num[there]]),
                     (edge_scale_out.at[num[side]], edge_scale_in.at[num[there]])]
        return [
            pltpu.make_async_remote_copy(
                src_ref=src, dst_ref=dst, send_sem=halo_send.at[num[side] // 2],
                recv_sem=halo_recv.at[num[side] // 2], device_id=near[side], device_id_type=MESH)
            for src, dst in pairs
        ]

    def halo_wait(sem):
        for axis, (low, high) in enumerate(("lr", "ud")):
            count = has[low].astype(jnp.int32) + has[high].astype(jnp.int32)
            for c in (1, 2):
                whole = (edge_tally.at[pl.ds(0, c)], wext.at[pl.ds(R, Y), pl.ds(0, 8 * c), :])[axis]

                @pl.when(count == c)
                def _():
                    pltpu.make_async_copy(whole, whole, sem.at[axis]).wait()

    lower = me + has["l"].astype(jnp.int32) + has["u"].astype(jnp.int32)

    @pl.when(lower > 0)
    def _():
        pl.semaphore_wait(barrier, lower)
    for t in range(n - 1, 0, -1):
        @pl.when(me - t >= 0)
        def _():
            pl.semaphore_signal(ready.at[me - 1], inc=1, device_id=far(me - t), device_id_type=MESH)
    for side in "lu":
        @pl.when(has[side])
        def _():
            pl.semaphore_signal(near_ready.at[0], inc=1, device_id=near[side], device_id_type=MESH)

    @pl.when(has["u"])
    def _():
        for copy in halo_copies("u"):
            copy.start()

    tiles = X // LANES

    def encode(total, whole_ref, scale_ref, *at):
        top = jnp.max(jnp.abs(total), axis=(0, 1))[None]
        top = functools.reduce(
            jnp.maximum, [top[:, q * LANES : (q + 1) * LANES] for q in range(tiles)])
        scale_ref[at] = top * (1.0 / TOP)
        up = jnp.concatenate([jnp.where(top > 0.0, TOP / top, 0.0)] * tiles, axis=1)
        whole = jnp.round(jnp.clip(total * up[None], -TOP, TOP)).astype(jnp.int32)
        whole_ref[at] = whole.astype(jnp.int16)

    def decode(whole_ref, scale_ref, *at):
        down = jnp.concatenate([scale_ref[at]] * tiles, axis=1)
        return whole_ref[at].astype(jnp.int32).astype(jnp.float32) * down[None]

    ld_bg.wait()
    for y in range(Y):
        bg[me, y] = pltpu.roll(raw[y].astype(jnp.float32), half, 1).astype(jnp.bfloat16)

    def piece_of(j, c):
        return bg.at[j, pl.ds(c * step, step)]

    def place(j, g):
        return j - (j > g).astype(jnp.int32)

    def bg_copy(j, c, target, slot, send):
        return pltpu.make_async_remote_copy(
            src_ref=piece_of(j, c), dst_ref=piece_of(j, c), send_sem=send,
            recv_sem=bg_recv.at[slot * pieces + c], device_id=target, device_id_type=MESH)

    def bg_sent(sem, count, most):
        for c in range(1, most):
            whole = bg.at[pl.ds(0, c)]

            @pl.when(count == c)
            def _():
                pltpu.make_async_copy(whole, whole, sem).wait()

    def relayed(j, g, core):
        left = jnp.logical_and(g == 0, j >= 3)
        right = jnp.logical_and(g >= j + 2, j >= 1)
        return jnp.where(g < j, left, right)

    def relay(j):
        onward = jnp.where(j < me, me + 1, me - 1)
        ok = jnp.logical_and(onward >= 0, onward < n)
        return onward, jnp.logical_and(ok, relayed(j, onward, other_shot))

    def direct(g):
        ok = jnp.logical_and(g >= 0, g < n)
        return jnp.logical_and(ok, jnp.logical_not(relayed(me, g, shot)))

    def send_own(g):
        for c in range(pieces):
            bg_copy(me, c, far(g), place(me, g), bg_send.at[0]).start()

    for t in range(n - 1, 0, -1):
        @pl.when(direct(me - t))
        def _():
            send_own(me - t)

    ld_now.wait()
    for side in "lr":
        encode(wext[mine[side], pl.ds(8, Z), :], edge_out, edge_scale_out, num[side])

    @pl.when(has["l"])
    def _():
        for copy in halo_copies("l"):
            copy.start()

    lead = lax.broadcasted_iota(jnp.int32, (2 * LANES, LANES), 0) - lax.broadcasted_iota(
        jnp.int32, (2 * LANES, LANES), 1)
    ld_off.wait()
    for k in range(K):
        move = 2 * half - off_ref[k]
        shift[k // 2, :, pl.ds(k % 2 * LANES, LANES)] = jnp.where(
            lead == move, 1.0, 0.0).astype(jnp.bfloat16)

    lane = lax.broadcasted_iota(jnp.int32, (step * Z, LANES), 1)

    def partial(j, c):
        rows = bg[j, pl.ds(c * step, step)].reshape(step * Z, X)
        cols = [rows[:, q * LANES : (q + 1) * LANES] for q in range(tiles)]
        zero = jnp.zeros_like(cols[0])
        cols.append(jnp.where(lane < half, cols[0], zero))
        cols[0] = jnp.where(lane < half, zero, cols[0])
        lhs = jnp.concatenate(
            [jnp.concatenate([cols[q], cols[q + 1]], axis=1) for q in range(tiles)], axis=0)
        total = None
        for k in range(K):
            if k % 2 == 0:
                moved = jnp.dot(lhs, shift[k // 2], preferred_element_type=jnp.float32)
            side = moved[:, k % 2 * LANES : (k % 2 + 1) * LANES]
            line = jnp.concatenate(
                [side[q * step * Z : (q + 1) * step * Z] for q in range(tiles)], axis=1)
            term = img[k, pl.ds(j * Y + c * step, step)].astype(jnp.float32) * line.reshape(step, Z, X)
            total = term if total is None else total + term
        return total

    joins = jnp.logical_and(me >= 1, me < n - 1)

    def part_send(j, c):
        def copies(dsts, recv, target):
            for src, dst in zip((part_out, scale_out), dsts):
                pltpu.make_async_remote_copy(
                    src_ref=src.at[j, c], dst_ref=dst, send_sem=p_send.at[0],
                    recv_sem=recv, device_id=target, device_id_type=MESH).start()

        @pl.when(j == me + 2)
        def _():
            copies((join_in.at[c], join_scale.at[c]), join_recv.at[c], {"off": me + 1})

        @pl.when(j != me + 2)
        def _():
            copies((part_in.at[me, c], scale_in.at[me, c]), p_recv.at[place(me, j)], far(j))

    img_load(me).wait()
    for c in range(pieces):
        acc[pl.ds(c * step, step)] = partial(me, c)

    for t in range(1, n):
        @pl.when(direct(me + t))
        def _():
            pl.semaphore_wait(ready.at[me + t - 1], 1)
            send_own(me + t)

    higher = has["r"].astype(jnp.int32) + has["d"].astype(jnp.int32)

    @pl.when(higher > 0)
    def _():
        pl.semaphore_wait(near_ready.at[0], higher)
    for side in "rd":
        @pl.when(has[side])
        def _():
            for copy in halo_copies(side):
                copy.start()

    rest = img.at[:, pl.ds(0, (n - 1) * Y)]
    pltpu.make_async_copy(rest, rest, img_sem.at[1]).wait()

    def laplace():
        ld_local.wait()
        halo_wait(halo_recv)
        for side in "lr":
            @pl.when(has[side])
            def _():
                wext[edge[side][0], edge[side][1], :] = decode(edge_in, edge_scale_in, num[side])

        wide = lax.broadcasted_iota(jnp.int32, (Z, X), 1)

        def plane(y, carry):
            centre = wext[y + R, pl.ds(8, Z), :]
            running = 3.0 * STENCIL[0] * centre
            for r in range(1, R + 1):
                beside = wext[y + R + r, pl.ds(8, Z), :] + wext[y + R - r, pl.ds(8, Z), :]
                beside = beside + wext[y + R, pl.ds(8 + r, Z), :]
                beside = beside + wext[y + R, pl.ds(8 - r, Z), :]
                beside = beside + jnp.where(wide < X - r, pltpu.roll(centre, X - r, 1), 0.0)
                beside = beside + jnp.where(wide >= r, pltpu.roll(centre, r, 1), 0.0)
                running = running + STENCIL[r] * beside
            fin[y] = 2.0 * centre - prev[y] + cour[y] * (running + acc[y])
            return carry

        lax.fori_loop(0, Y, plane, 0)

    early = jnp.logical_and(jnp.logical_and(me >= 2, me < n - 1), shot == 0)

    @pl.loop(0, (n - 1) * pieces)
    def _(q):
        swap = jnp.where(q == 0, pieces, jnp.where(q <= pieces, q - 1, q))
        turns = jnp.where(q == 1, 2, jnp.where(q == 2, 1, q)) if pieces == 2 and n > 2 else q
        q = jnp.where(early, swap, jnp.where(me == 1, turns, q))
        i, c = q // pieces, q % pieces
        j = order(i)

        @pl.when(jnp.logical_and(me == 0, q == (n - 2) * pieces))
        def _():
            laplace()

        onward, go_on = relay(j)
        bg_copy(j, c, far(j), place(j, me), bg_send.at[0]).wait_recv()

        @pl.when(go_on)
        def _():
            bg_copy(j, c, {"off": onward}, place(j, onward), bg_send.at[1]).start()

        @pl.when(jnp.logical_and(c == 0, jnp.logical_and(j > me, relayed(me, j, shot))))
        def _():
            pl.semaphore_wait(ready.at[j - 1], 1)
        total = partial(j, c)
        later = jnp.logical_and(joins, j == me + 1)

        @pl.when(later)
        def _():
            pend[pl.ds(c * step, step)] = total

        @pl.when(jnp.logical_not(later))
        def _():
            encode(total, part_out, scale_out, j, c)
            part_send(j, c)

    @pl.when(joins)
    def _():
        for c in range(pieces):
            pltpu.make_async_copy(piece_tally, piece_tally, join_recv.at[c]).wait()
            total = pend[pl.ds(c * step, step)] + decode(join_in, join_scale, c)
            encode(total, part_out, scale_out, me + 1, c)
            part_send(me + 1, c)

    @pl.when(me > 0)
    def _():
        laplace()

    def drain():
        halo_wait(halo_send)
        sent, passed = 0, 0
        for g in range(n):
          there = g != me
          sent = sent + jnp.logical_and(there, direct(g)).astype(jnp.int32)
          passed = passed + jnp.logical_and(there, relay(g)[1]).astype(jnp.int32)
        bg_sent(bg_send.at[0], sent, n)
        bg_sent(bg_send.at[1], passed, n - 1)
        pltpu.make_async_copy(tally, tally, p_send.at[0]).wait()

    @pl.loop(0, n - 1)
    def _(i):
        j = order(i)

        @pl.when(i == n - 2)
        def _():
            drain()

        @pl.when(j != me - 2)
        def _():
            pltpu.make_async_copy(tally.at[0], tally.at[0], p_recv.at[place(j, me)]).wait()
            for c in range(pieces):
                rows = pl.ds(c * step, step)
                fin[rows] = fin[rows] + cour[rows] * decode(part_in, scale_in, j, c)


def on_device(n, nd, image, offset_of, background, wave_now, wave_prev, courant):
    K, rows, Z, X = image.shape
    Y = wave_now.shape[1]
    f32 = jnp.float32
    pieces = PIECES if Y % PIECES == 0 else 1
    step = Y // pieces
    lines = (Y * Z * X * 2) // (LANES * 4) + pieces
    dma = pltpu.SemaphoreType.DMA
    regular = pltpu.SemaphoreType.REGULAR
    return pl.pallas_call(
        functools.partial(kernel, n, nd),
        out_shape=jax.ShapeDtypeStruct(wave_now.shape, f32),
        in_specs=[pl.BlockSpec(memory_space=pltpu.HBM)] * 6,
        out_specs=pl.BlockSpec(memory_space=pltpu.VMEM),
        scratch_shapes=[
            pltpu.SMEM((K,), jnp.int32),
            pltpu.VMEM((K, rows, Z, X), jnp.bfloat16),
            pltpu.VMEM((Y, Z, X), jnp.bfloat16),
            pltpu.VMEM((n, Y, Z, X), jnp.bfloat16),
            pltpu.VMEM((Y + 2 * R, Z + 16, X), f32),
            pltpu.VMEM((2, Y, Z, X), f32),
            pltpu.VMEM(((K + 1) // 2, 2 * LANES, 2 * LANES), jnp.bfloat16),
            pltpu.VMEM((Y, Z, X), f32),
            pltpu.VMEM((n, pieces, step, Z, X), jnp.int16),
            pltpu.VMEM((n, pieces, step, Z, X), jnp.int16),
            pltpu.VMEM((n, pieces, 1, LANES), f32),
            pltpu.VMEM((n, pieces, 1, LANES), f32),
            pltpu.VMEM((Y, Z, X), f32),
            pltpu.VMEM((pieces, step, Z, X), jnp.int16),
            pltpu.VMEM((pieces, 1, LANES), f32),
            pltpu.VMEM((n - 1, lines, LANES), f32),
            pltpu.VMEM((2, R, Z, X), jnp.int16),
            pltpu.VMEM((2, R, Z, X), jnp.int16),
            pltpu.VMEM((2, 1, LANES), f32),
            pltpu.VMEM((2, 1, LANES), f32),
            pltpu.VMEM((2, (R * Z * X * 2) // (LANES * 4) + 1, LANES), f32),
            pltpu.VMEM((lines // pieces, LANES), f32),
            dma((4,)), dma((2,)), regular((n - 1,)), regular((1,)),
            dma(((n - 1) * pieces,)), dma((2,)), dma((2,)), dma((2,)),
            dma((n - 1,)), dma((pieces,)), dma((1,)),
        ],
        compiler_params=pltpu.CompilerParams(
            collective_id=0, has_side_effects=True, vmem_limit_bytes=50331648),
        name="born_step",
    )(*[pltpu.with_memory_space_constraint(a, pltpu.HBM) for a in
        (offset_of, image, background, wave_now, wave_prev, courant)])


def solution(mesh):
    wave = P(("parts", "shot"), "off", "depth", None)
    return jax.shard_map(
        functools.partial(on_device, mesh.shape["off"], mesh.shape["depth"]),
        mesh=mesh,
        in_specs=(
            P("off", None, "depth", None),
            P("off"),
            wave,
            wave,
            wave,
            P("off", "depth", None),
        ),
        out_specs=wave,
        check_vma=False,
    )
```

```python
import functools

import jax
import jax.numpy as jnp
from jax import lax
from jax.experimental import pallas as pl
from jax.experimental.pallas import tpu as pltpu
from jax.sharding import PartitionSpec as P

STENCIL = (-205.0 / 72.0, 8.0 / 5.0, -1.0 / 5.0, 8.0 / 315.0, -1.0 / 560.0)
R = 4
LANES = 128
TOP = 32767.0
PIECES = 2
MESH = pl.DeviceIdType.MESH


def kernel(
    n, nd,
    off_hbm, img_hbm, bg_hbm, now_hbm, prev_hbm, cour_hbm,
    out_ref,
    off_ref, img, raw, bg, wext, local, shift, acc,
    part_out, part_in, scale_out, scale_in, pend, join_in, join_scale, tally,
    edge_out, edge_in, edge_scale_out, edge_scale_in, edge_tally, piece_tally,
    load_sem, img_sem, ready, near_ready, bg_recv, bg_send,
    halo_send, halo_recv, p_recv, join_recv, p_send,
):
    K, _, Z, X = img.shape
    Y = out_ref.shape[1]
    step = part_out.shape[2]
    pieces = part_out.shape[1]
    half = K * n // 2
    me = lax.axis_index("off")
    dep = lax.axis_index("depth")
    shot = lax.axis_index("shot")
    other_shot = lax.axis_size("shot") - 1 - shot
    has = {"l": me > 0, "r": me < n - 1, "u": dep > 0, "d": dep < nd - 1}
    near = {"l": {"off": me - 1}, "r": {"off": me + 1},
            "u": {"depth": dep - 1}, "d": {"depth": dep + 1}}
    fin = out_ref.at[0]

    def far(j):
        return {"off": j, "shot": other_shot}

    ld_bg = pltpu.make_async_copy(bg_hbm.at[0], raw, load_sem.at[0])
    ld_off = pltpu.make_async_copy(off_hbm, off_ref, load_sem.at[1])
    ld_now = pltpu.make_async_copy(
        now_hbm.at[0], wext.at[pl.ds(R, Y), pl.ds(8, Z), :], load_sem.at[2])
    prev, cour = local.at[0], local.at[1]
    ld_prev = pltpu.make_async_copy(prev_hbm.at[0], prev, load_sem.at[3])
    ld_cour = pltpu.make_async_copy(cour_hbm, cour, load_sem.at[3])
    ld_local = pltpu.make_async_copy(local, local, load_sem.at[3])
    ld_bg.start()
    ld_off.start()
    ld_now.start()

    barrier = pltpu.get_barrier_semaphore()
    for t in range(1, n):
        @pl.when(me + t < n)
        def _():
            pl.semaphore_signal(barrier, inc=1, device_id=far(me + t), device_id_type=MESH)
    for side in "rd":
        @pl.when(has[side])
        def _():
            pl.semaphore_signal(barrier, inc=1, device_id=near[side], device_id_type=MESH)

    def img_load(j):
        rows = pl.ds(j * Y, Y)
        sem = img_sem.at[jnp.where(j == me, 0, 1)]
        return pltpu.make_async_copy(img_hbm.at[:, rows], img.at[:, rows], sem)

    def order(i):
        mid = jnp.where(i == 0, 0, jnp.where(i == 1, n - 1, i))
        rest = jnp.where(i < me, i - 1, i + 1)
        last = me == n - 1
        first = jnp.where(last, me - 1, 0)
        second = jnp.where(last, 0, me - 1)
        high = jnp.where(i == 0, first, jnp.where(i == 1, second, rest))
        low = jnp.where(i == 0, 2, jnp.where(i == 1, 1, i + 1))
        return jnp.where(me == 0, low, jnp.where(me == 1, mid, high))

    img_load(me).start()

    @pl.loop(0, n - 1)
    def _(i):
        img_load(order(i)).start()

    ld_prev.start()
    ld_cour.start()

    def clear(rows, cols):
        wext[rows, cols, :] = jnp.zeros((rows.size, cols.size, X), jnp.float32)

    edge = {"l": (pl.ds(0, R), pl.ds(8, Z)), "r": (pl.ds(R + Y, R), pl.ds(8, Z)),
            "u": (pl.ds(R, Y), pl.ds(0, 8)), "d": (pl.ds(R, Y), pl.ds(8 + Z, 8))}
    for side in "lrud":
        @pl.when(jnp.logical_not(has[side]))
        def _():
            clear(*edge[side])

    mine = {"l": pl.ds(R, R), "r": pl.ds(Y, R), "u": pl.ds(0, 8), "d": pl.ds(Z - 8, 8)}
    other = {"l": "r", "r": "l", "u": "d", "d": "u"}
    num = {"l": 0, "r": 1, "u": 2, "d": 3}

    def halo_copies(side):
        there = other[side]
        if side in "ud":
            pairs = [(now_hbm.at[0, :, mine[side], :], wext.at[edge[there][0], edge[there][1], :])]
        else:
            pairs = [(edge_out.at[num[side]], edge_in.at[num[there]]),
                     (edge_scale_out.at[num[side]], edge_scale_in.at[num[there]])]
        return [
            pltpu.make_async_remote_copy(
                src_ref=src, dst_ref=dst, send_sem=halo_send.at[num[side] // 2],
                recv_sem=halo_recv.at[num[side] // 2], device_id=near[side], device_id_type=MESH)
            for src, dst in pairs
        ]

    def halo_wait(sem):
        for axis, (low, high) in enumerate(("lr", "ud")):
            count = has[low].astype(jnp.int32) + has[high].astype(jnp.int32)
            for c in (1, 2):
                whole = (edge_tally.at[pl.ds(0, c)], wext.at[pl.ds(R, Y), pl.ds(0, 8 * c), :])[axis]

                @pl.when(count == c)
                def _():
                    pltpu.make_async_copy(whole, whole, sem.at[axis]).wait()

    lower = me + has["l"].astype(jnp.int32) + has["u"].astype(jnp.int32)

    @pl.when(lower > 0)
    def _():
        pl.semaphore_wait(barrier, lower)
    for t in range(n - 1, 0, -1):
        @pl.when(me - t >= 0)
        def _():
            pl.semaphore_signal(ready.at[me - 1], inc=1, device_id=far(me - t), device_id_type=MESH)
    for side in "lu":
        @pl.when(has[side])
        def _():
            pl.semaphore_signal(near_ready.at[0], inc=1, device_id=near[side], device_id_type=MESH)

    @pl.when(has["u"])
    def _():
        for copy in halo_copies("u"):
            copy.start()

    tiles = X // LANES

    def encode(total, whole_ref, scale_ref, *at):
        top = jnp.max(jnp.abs(total), axis=(0, 1))[None]
        top = functools.reduce(
            jnp.maximum, [top[:, q * LANES : (q + 1) * LANES] for q in range(tiles)])
        scale_ref[at] = top * (1.0 / TOP)
        up = jnp.concatenate([jnp.where(top > 0.0, TOP / top, 0.0)] * tiles, axis=1)
        whole = jnp.round(jnp.clip(total * up[None], -TOP, TOP)).astype(jnp.int32)
        whole_ref[at] = whole.astype(jnp.int16)

    def decode(whole_ref, scale_ref, *at):
        down = jnp.concatenate([scale_ref[at]] * tiles, axis=1)
        return whole_ref[at].astype(jnp.int32).astype(jnp.float32) * down[None]

    ld_bg.wait()
    for y in range(Y):
        bg[me, y] = pltpu.roll(raw[y].astype(jnp.float32), half, 1).astype(jnp.bfloat16)

    def piece_of(j, c):
        return bg.at[j, pl.ds(c * step, step)]

    def place(j, g):
        return j - (j > g).astype(jnp.int32)

    def bg_copy(j, c, target, slot, send):
        return pltpu.make_async_remote_copy(
            src_ref=piece_of(j, c), dst_ref=piece_of(j, c), send_sem=send,
            recv_sem=bg_recv.at[slot * pieces + c], device_id=target, device_id_type=MESH)

    def bg_sent(sem, count, most):
        for c in range(1, most):
            whole = bg.at[pl.ds(0, c)] if c <= n else img.at[pl.ds(0, 2), pl.ds(0, c * Y // 2)]

            @pl.when(count == c)
            def _():
                pltpu.make_async_copy(whole, whole, sem).wait()

    def relayed(j, g, core):
        left = jnp.logical_and(g == 0, j >= 3)
        right = jnp.logical_and(g >= j + 2, j >= 1)
        return jnp.where(g < j, left, right)

    def relay(j):
        onward = jnp.where(j < me, me + 1, me - 1)
        ok = jnp.logical_and(onward >= 0, onward < n)
        return onward, jnp.logical_and(ok, relayed(j, onward, other_shot))

    def direct(g):
        ok = jnp.logical_and(g >= 0, g < n)
        return jnp.logical_and(ok, jnp.logical_not(relayed(me, g, shot)))

    def send_own(g):
        for c in range(pieces):
            bg_copy(me, c, far(g), place(me, g), bg_send.at[0]).start()

    for t in range(n - 1, 0, -1):
        @pl.when(direct(me - t))
        def _():
            send_own(me - t)

    ld_now.wait()
    for side in "lr":
        encode(wext[mine[side], pl.ds(8, Z), :], edge_out, edge_scale_out, num[side])

    @pl.when(has["l"])
    def _():
        for copy in halo_copies("l"):
            copy.start()

    lead = lax.broadcasted_iota(jnp.int32, (2 * LANES, LANES), 0) - lax.broadcasted_iota(
        jnp.int32, (2 * LANES, LANES), 1)
    ld_off.wait()
    for k in range(K):
        move = 2 * half - off_ref[k]
        shift[k // 2, :, pl.ds(k % 2 * LANES, LANES)] = jnp.where(
            lead == move, 1.0, 0.0).astype(jnp.bfloat16)

    lane = lax.broadcasted_iota(jnp.int32, (step * Z, LANES), 1)

    def partial(j, c):
        rows = bg[j, pl.ds(c * step, step)].reshape(step * Z, X)
        cols = [rows[:, q * LANES : (q + 1) * LANES] for q in range(tiles)]
        zero = jnp.zeros_like(cols[0])
        cols.append(jnp.where(lane < half, cols[0], zero))
        cols[0] = jnp.where(lane < half, zero, cols[0])
        lhs = jnp.concatenate(
            [jnp.concatenate([cols[q], cols[q + 1]], axis=1) for q in range(tiles)], axis=0)
        total = None
        for k in range(K):
            if k % 2 == 0:
                moved = jnp.dot(lhs, shift[k // 2], preferred_element_type=jnp.float32)
            side = moved[:, k % 2 * LANES : (k % 2 + 1) * LANES]
            line = jnp.concatenate(
                [side[q * step * Z : (q + 1) * step * Z] for q in range(tiles)], axis=1)
            term = img[k, pl.ds(j * Y + c * step, step)].astype(jnp.float32) * line.reshape(step, Z, X)
            total = term if total is None else total + term
        return total

    joins = jnp.logical_and(me >= 1, me < n - 1)

    def part_send(j, c):
        def copies(dsts, recv, target):
            for src, dst in zip((part_out, scale_out), dsts):
                pltpu.make_async_remote_copy(
                    src_ref=src.at[j, c], dst_ref=dst, send_sem=p_send.at[0],
                    recv_sem=recv, device_id=target, device_id_type=MESH).start()

        @pl.when(j == me + 2)
        def _():
            copies((join_in.at[c], join_scale.at[c]), join_recv.at[c], {"off": me + 1})

        @pl.when(j != me + 2)
        def _():
            copies((part_in.at[me, c], scale_in.at[me, c]), p_recv.at[place(me, j)], far(j))

    img_load(me).wait()
    for c in range(pieces):
        acc[pl.ds(c * step, step)] = partial(me, c)

    for t in range(1, n):
        @pl.when(direct(me + t))
        def _():
            pl.semaphore_wait(ready.at[me + t - 1], 1)
            send_own(me + t)

    higher = has["r"].astype(jnp.int32) + has["d"].astype(jnp.int32)

    @pl.when(higher > 0)
    def _():
        pl.semaphore_wait(near_ready.at[0], higher)
    for side in "rd":
        @pl.when(has[side])
        def _():
            for copy in halo_copies(side):
                copy.start()

    rest = img.at[:, pl.ds(0, (n - 1) * Y)]
    pltpu.make_async_copy(rest, rest, img_sem.at[1]).wait()

    def laplace():
        ld_local.wait()
        halo_wait(halo_recv)
        for side in "lr":
            @pl.when(has[side])
            def _():
                wext[edge[side][0], edge[side][1], :] = decode(edge_in, edge_scale_in, num[side])

        wide = lax.broadcasted_iota(jnp.int32, (Z, X), 1)

        def plane(y, carry):
            centre = wext[y + R, pl.ds(8, Z), :]
            running = 3.0 * STENCIL[0] * centre
            for r in range(1, R + 1):
                beside = wext[y + R + r, pl.ds(8, Z), :] + wext[y + R - r, pl.ds(8, Z), :]
                beside = beside + wext[y + R, pl.ds(8 + r, Z), :]
                beside = beside + wext[y + R, pl.ds(8 - r, Z), :]
                beside = beside + jnp.where(wide < X - r, pltpu.roll(centre, X - r, 1), 0.0)
                beside = beside + jnp.where(wide >= r, pltpu.roll(centre, r, 1), 0.0)
                running = running + STENCIL[r] * beside
            fin[y] = 2.0 * centre - prev[y] + cour[y] * (running + acc[y])
            return carry

        lax.fori_loop(0, Y, plane, 0)

    early = jnp.logical_and(jnp.logical_and(me >= 2, me < n - 1), shot == 0)

    @pl.loop(0, (n - 1) * pieces)
    def _(q):
        swap = jnp.where(q == 0, pieces, jnp.where(q <= pieces, q - 1, q))
        turns = q
        if pieces == 2 and n > 2:
            turns = jnp.where(shot == 0, jnp.where(q < 4, (q // 2) + 2 * (1 - q % 2), q), q)
        q = jnp.where(early, swap, jnp.where(me == 1, turns, q))
        i, c = q // pieces, q % pieces
        j = order(i)

        @pl.when(jnp.logical_and(me == 0, q == (n - 2) * pieces))
        def _():
            laplace()

        onward, go_on = relay(j)
        bg_copy(j, c, far(j), place(j, me), bg_send.at[0]).wait_recv()

        @pl.when(go_on)
        def _():
            bg_copy(j, c, {"off": onward}, place(j, onward), bg_send.at[0]).start()

        @pl.when(jnp.logical_and(c == 0, jnp.logical_and(j > me, relayed(me, j, shot))))
        def _():
            pl.semaphore_wait(ready.at[j - 1], 1)
        total = partial(j, c)
        later = jnp.logical_and(joins, j == me + 1)

        @pl.when(later)
        def _():
            pend[pl.ds(c * step, step)] = total

        @pl.when(jnp.logical_not(later))
        def _():
            encode(total, part_out, scale_out, j, c)
            part_send(j, c)

    @pl.when(joins)
    def _():
        for c in range(pieces):
            pltpu.make_async_copy(piece_tally, piece_tally, join_recv.at[c]).wait()
            total = pend[pl.ds(c * step, step)] + decode(join_in, join_scale, c)
            encode(total, part_out, scale_out, me + 1, c)
            part_send(me + 1, c)

    @pl.when(me > 0)
    def _():
        laplace()

    def drain():
        halo_wait(halo_send)
        sent, passed = 0, 0
        for g in range(n):
          there = g != me
          sent = sent + jnp.logical_and(there, direct(g)).astype(jnp.int32)
          passed = passed + jnp.logical_and(there, relay(g)[1]).astype(jnp.int32)
        bg_sent(bg_send.at[0], sent + passed, 2 * n)
        pltpu.make_async_copy(tally, tally, p_send.at[0]).wait()

    @pl.loop(0, n - 1)
    def _(i):
        j = order(i)

        @pl.when(i == n - 2)
        def _():
            drain()

        @pl.when(j != me - 2)
        def _():
            pltpu.make_async_copy(tally.at[0], tally.at[0], p_recv.at[place(j, me)]).wait()
            for c in range(pieces):
                rows = pl.ds(c * step, step)
                fin[rows] = fin[rows] + cour[rows] * decode(part_in, scale_in, j, c)


def on_device(n, nd, image, offset_of, background, wave_now, wave_prev, courant):
    K, rows, Z, X = image.shape
    Y = wave_now.shape[1]
    f32 = jnp.float32
    pieces = PIECES if Y % PIECES == 0 else 1
    step = Y // pieces
    lines = (Y * Z * X * 2) // (LANES * 4) + pieces
    dma = pltpu.SemaphoreType.DMA
    regular = pltpu.SemaphoreType.REGULAR
    return pl.pallas_call(
        functools.partial(kernel, n, nd),
        out_shape=jax.ShapeDtypeStruct(wave_now.shape, f32),
        in_specs=[pl.BlockSpec(memory_space=pltpu.HBM)] * 6,
        out_specs=pl.BlockSpec(memory_space=pltpu.VMEM),
        scratch_shapes=[
            pltpu.SMEM((K,), jnp.int32),
            pltpu.VMEM((K, rows, Z, X), jnp.bfloat16),
            pltpu.VMEM((Y, Z, X), jnp.bfloat16),
            pltpu.VMEM((n, Y, Z, X), jnp.bfloat16),
            pltpu.VMEM((Y + 2 * R, Z + 16, X), f32),
            pltpu.VMEM((2, Y, Z, X), f32),
            pltpu.VMEM(((K + 1) // 2, 2 * LANES, 2 * LANES), jnp.bfloat16),
            pltpu.VMEM((Y, Z, X), f32),
            pltpu.VMEM((n, pieces, step, Z, X), jnp.int16),
            pltpu.VMEM((n, pieces, step, Z, X), jnp.int16),
            pltpu.VMEM((n, pieces, 1, LANES), f32),
            pltpu.VMEM((n, pieces, 1, LANES), f32),
            pltpu.VMEM((Y, Z, X), f32),
            pltpu.VMEM((pieces, step, Z, X), jnp.int16),
            pltpu.VMEM((pieces, 1, LANES), f32),
            pltpu.VMEM((n - 1, lines, LANES), f32),
            pltpu.VMEM((2, R, Z, X), jnp.int16),
            pltpu.VMEM((2, R, Z, X), jnp.int16),
            pltpu.VMEM((2, 1, LANES), f32),
            pltpu.VMEM((2, 1, LANES), f32),
            pltpu.VMEM((2, (R * Z * X * 2) // (LANES * 4) + 1, LANES), f32),
            pltpu.VMEM((lines // pieces, LANES), f32),
            dma((4,)), dma((2,)), regular((n - 1,)), regular((1,)),
            dma(((n - 1) * pieces,)), dma((1,)), dma((2,)), dma((2,)),
            dma((n - 1,)), dma((pieces,)), dma((1,)),
        ],
        compiler_params=pltpu.CompilerParams(
            collective_id=0, has_side_effects=True, vmem_limit_bytes=50331648),
        name="born_step",
    )(*[pltpu.with_memory_space_constraint(a, pltpu.HBM) for a in
        (offset_of, image, background, wave_now, wave_prev, courant)])


def solution(mesh):
    wave = P(("parts", "shot"), "off", "depth", None)
    return jax.shard_map(
        functools.partial(on_device, mesh.shape["off"], mesh.shape["depth"]),
        mesh=mesh,
        in_specs=(
            P("off", None, "depth", None),
            P("off"),
            wave,
            wave,
            wave,
            P("off", "depth", None),
        ),
        out_specs=wave,
        check_vma=False,
    )
```

```python
import functools

import jax
import jax.numpy as jnp
from jax import lax
from jax.experimental import pallas as pl
from jax.experimental.pallas import tpu as pltpu
from jax.sharding import PartitionSpec as P

STENCIL = (-205.0 / 72.0, 8.0 / 5.0, -1.0 / 5.0, 8.0 / 315.0, -1.0 / 560.0)
R = 4
LANES = 128
TOP = 32767.0
PIECES = 2
MESH = pl.DeviceIdType.MESH


def kernel(
    n, nd,
    off_hbm, img_hbm, bg_hbm, now_hbm, prev_hbm, cour_hbm,
    out_ref,
    off_ref, img, raw, bg, wext, local, shift, acc,
    part_out, part_in, scale_out, scale_in, pend, join_in, join_scale, tally,
    edge_out, edge_in, edge_scale_out, edge_scale_in, edge_tally, piece_tally,
    load_sem, img_sem, ready, near_ready, bg_recv, bg_send,
    halo_send, halo_recv, p_recv, join_recv, p_send,
):
    K, _, Z, X = img.shape
    Y = out_ref.shape[1]
    step = part_out.shape[2]
    pieces = part_out.shape[1]
    half = K * n // 2
    me = lax.axis_index("off")
    dep = lax.axis_index("depth")
    shot = lax.axis_index("shot")
    other_shot = lax.axis_size("shot") - 1 - shot
    has = {"l": me > 0, "r": me < n - 1, "u": dep > 0, "d": dep < nd - 1}
    near = {"l": {"off": me - 1}, "r": {"off": me + 1},
            "u": {"depth": dep - 1}, "d": {"depth": dep + 1}}
    fin = out_ref.at[0]

    def far(j):
        return {"off": j, "shot": other_shot}

    ld_bg = pltpu.make_async_copy(bg_hbm.at[0], raw, load_sem.at[0])
    ld_off = pltpu.make_async_copy(off_hbm, off_ref, load_sem.at[1])
    ld_now = pltpu.make_async_copy(
        now_hbm.at[0], wext.at[pl.ds(R, Y), pl.ds(8, Z), :], load_sem.at[2])
    prev, cour = local.at[0], local.at[1]
    ld_prev = pltpu.make_async_copy(prev_hbm.at[0], prev, load_sem.at[3])
    ld_cour = pltpu.make_async_copy(cour_hbm, cour, load_sem.at[3])
    ld_local = pltpu.make_async_copy(local, local, load_sem.at[3])
    ld_bg.start()
    ld_off.start()
    ld_now.start()

    barrier = pltpu.get_barrier_semaphore()
    for t in range(1, n):
        @pl.when(me + t < n)
        def _():
            pl.semaphore_signal(barrier, inc=1, device_id=far(me + t), device_id_type=MESH)
    for side in "rd":
        @pl.when(has[side])
        def _():
            pl.semaphore_signal(barrier, inc=1, device_id=near[side], device_id_type=MESH)

    def img_load(j):
        rows = pl.ds(j * Y, Y)
        sem = img_sem.at[jnp.where(j == me, 0, 1)]
        return pltpu.make_async_copy(img_hbm.at[:, rows], img.at[:, rows], sem)

    def order(i):
        mid = jnp.where(i == 0, 0, jnp.where(i == 1, n - 1, i))
        rest = jnp.where(i < me, i - 1, i + 1)
        last = me == n - 1
        first = jnp.where(last, me - 1, 0)
        second = jnp.where(last, 0, me - 1)
        high = jnp.where(i == 0, first, jnp.where(i == 1, second, rest))
        low = jnp.where(i == 0, 2, jnp.where(i == 1, 1, i + 1))
        return jnp.where(me == 0, low, jnp.where(me == 1, mid, high))

    img_load(me).start()

    @pl.loop(0, n - 1)
    def _(i):
        img_load(order(i)).start()

    ld_prev.start()
    ld_cour.start()

    def clear(rows, cols):
        wext[rows, cols, :] = jnp.zeros((rows.size, cols.size, X), jnp.float32)

    edge = {"l": (pl.ds(0, R), pl.ds(8, Z)), "r": (pl.ds(R + Y, R), pl.ds(8, Z)),
            "u": (pl.ds(R, Y), pl.ds(0, 8)), "d": (pl.ds(R, Y), pl.ds(8 + Z, 8))}
    for side in "lrud":
        @pl.when(jnp.logical_not(has[side]))
        def _():
            clear(*edge[side])

    mine = {"l": pl.ds(R, R), "r": pl.ds(Y, R), "u": pl.ds(0, 8), "d": pl.ds(Z - 8, 8)}
    other = {"l": "r", "r": "l", "u": "d", "d": "u"}
    num = {"l": 0, "r": 1, "u": 2, "d": 3}

    def halo_copies(side):
        there = other[side]
        if side in "ud":
            pairs = [(now_hbm.at[0, :, mine[side], :], wext.at[edge[there][0], edge[there][1], :])]
        else:
            pairs = [(edge_out.at[num[side]], edge_in.at[num[there]]),
                     (edge_scale_out.at[num[side]], edge_scale_in.at[num[there]])]
        return [
            pltpu.make_async_remote_copy(
                src_ref=src, dst_ref=dst, send_sem=halo_send.at[num[side] // 2],
                recv_sem=halo_recv.at[num[side] // 2], device_id=near[side], device_id_type=MESH)
            for src, dst in pairs
        ]

    def halo_wait(sem):
        for axis, (low, high) in enumerate(("lr", "ud")):
            count = has[low].astype(jnp.int32) + has[high].astype(jnp.int32)
            for c in (1, 2):
                whole = (edge_tally.at[pl.ds(0, c)], wext.at[pl.ds(R, Y), pl.ds(0, 8 * c), :])[axis]

                @pl.when(count == c)
                def _():
                    pltpu.make_async_copy(whole, whole, sem.at[axis]).wait()

    lower = me + has["l"].astype(jnp.int32) + has["u"].astype(jnp.int32)

    @pl.when(lower > 0)
    def _():
        pl.semaphore_wait(barrier, lower)
    for t in range(n - 1, 0, -1):
        @pl.when(me - t >= 0)
        def _():
            pl.semaphore_signal(ready.at[me - 1], inc=1, device_id=far(me - t), device_id_type=MESH)
    for side in "lu":
        @pl.when(has[side])
        def _():
            pl.semaphore_signal(near_ready.at[0], inc=1, device_id=near[side], device_id_type=MESH)

    @pl.when(has["u"])
    def _():
        for copy in halo_copies("u"):
            copy.start()

    tiles = X // LANES

    def encode(total, whole_ref, scale_ref, *at):
        top = jnp.max(jnp.abs(total), axis=(0, 1))[None]
        top = functools.reduce(
            jnp.maximum, [top[:, q * LANES : (q + 1) * LANES] for q in range(tiles)])
        scale_ref[at] = top * (1.0 / TOP)
        up = jnp.concatenate([jnp.where(top > 0.0, TOP / top, 0.0)] * tiles, axis=1)
        whole = jnp.round(jnp.clip(total * up[None], -TOP, TOP)).astype(jnp.int32)
        whole_ref[at] = whole.astype(jnp.int16)

    def decode(whole_ref, scale_ref, *at):
        down = jnp.concatenate([scale_ref[at]] * tiles, axis=1)
        return whole_ref[at].astype(jnp.int32).astype(jnp.float32) * down[None]

    ld_bg.wait()
    for y in range(Y):
        bg[me, y] = pltpu.roll(raw[y].astype(jnp.float32), half, 1).astype(jnp.bfloat16)

    def piece_of(j, c):
        return bg.at[j, pl.ds(c * step, step)]

    def place(j, g):
        return j - (j > g).astype(jnp.int32)

    def bg_copy(j, c, target, slot, send):
        return pltpu.make_async_remote_copy(
            src_ref=piece_of(j, c), dst_ref=piece_of(j, c), send_sem=send,
            recv_sem=bg_recv.at[slot * pieces + c], device_id=target, device_id_type=MESH)

    def bg_sent(sem, count, most):
        for c in range(1, most):
            whole = bg.at[pl.ds(0, c)] if c <= n else img.at[pl.ds(0, 2), pl.ds(0, c * Y // 2)]

            @pl.when(count == c)
            def _():
                pltpu.make_async_copy(whole, whole, sem).wait()

    def relayed(j, g, core):
        left = jnp.logical_and(g == 0, j >= 3)
        right = jnp.logical_and(g >= j + 2, j >= 1)
        return jnp.where(g < j, left, right)

    def relay(j):
        onward = jnp.where(j < me, me + 1, me - 1)
        ok = jnp.logical_and(onward >= 0, onward < n)
        return onward, jnp.logical_and(ok, relayed(j, onward, other_shot))

    def direct(g):
        ok = jnp.logical_and(g >= 0, g < n)
        return jnp.logical_and(ok, jnp.logical_not(relayed(me, g, shot)))

    def send_own(g):
        for c in range(pieces):
            bg_copy(me, c, far(g), place(me, g), bg_send.at[0]).start()

    for t in range(n - 1, 0, -1):
        @pl.when(direct(me - t))
        def _():
            send_own(me - t)

    ld_now.wait()
    for side in "lr":
        encode(wext[mine[side], pl.ds(8, Z), :], edge_out, edge_scale_out, num[side])

    @pl.when(has["l"])
    def _():
        for copy in halo_copies("l"):
            copy.start()

    lead = lax.broadcasted_iota(jnp.int32, (2 * LANES, LANES), 0) - lax.broadcasted_iota(
        jnp.int32, (2 * LANES, LANES), 1)
    ld_off.wait()
    for k in range(K):
        move = 2 * half - off_ref[k]
        shift[k // 2, :, pl.ds(k % 2 * LANES, LANES)] = jnp.where(
            lead == move, 1.0, 0.0).astype(jnp.bfloat16)

    lane = lax.broadcasted_iota(jnp.int32, (step * Z, LANES), 1)

    def partial(j, c):
        rows = bg[j, pl.ds(c * step, step)].reshape(step * Z, X)
        cols = [rows[:, q * LANES : (q + 1) * LANES] for q in range(tiles)]
        zero = jnp.zeros_like(cols[0])
        cols.append(jnp.where(lane < half, cols[0], zero))
        cols[0] = jnp.where(lane < half, zero, cols[0])
        lhs = jnp.concatenate(
            [jnp.concatenate([cols[q], cols[q + 1]], axis=1) for q in range(tiles)], axis=0)
        total = None
        for k in range(K):
            if k % 2 == 0:
                moved = jnp.dot(lhs, shift[k // 2], preferred_element_type=jnp.float32)
            side = moved[:, k % 2 * LANES : (k % 2 + 1) * LANES]
            line = jnp.concatenate(
                [side[q * step * Z : (q + 1) * step * Z] for q in range(tiles)], axis=1)
            term = img[k, pl.ds(j * Y + c * step, step)].astype(jnp.float32) * line.reshape(step, Z, X)
            total = term if total is None else total + term
        return total

    joins = jnp.logical_and(me >= 1, me < n - 1)

    def part_send(j, c):
        def copies(dsts, recv, target):
            for src, dst in zip((part_out, scale_out), dsts):
                pltpu.make_async_remote_copy(
                    src_ref=src.at[j, c], dst_ref=dst, send_sem=p_send.at[0],
                    recv_sem=recv, device_id=target, device_id_type=MESH).start()

        @pl.when(j == me + 2)
        def _():
            copies((join_in.at[c], join_scale.at[c]), join_recv.at[c], {"off": me + 1})

        @pl.when(j != me + 2)
        def _():
            copies((part_in.at[me, c], scale_in.at[me, c]), p_recv.at[place(me, j)], far(j))

    img_load(me).wait()
    for c in range(pieces):
        acc[pl.ds(c * step, step)] = partial(me, c)

    for t in range(1, n):
        @pl.when(direct(me + t))
        def _():
            pl.semaphore_wait(ready.at[me + t - 1], 1)
            send_own(me + t)

    higher = has["r"].astype(jnp.int32) + has["d"].astype(jnp.int32)

    @pl.when(higher > 0)
    def _():
        pl.semaphore_wait(near_ready.at[0], higher)
    for side in "rd":
        @pl.when(has[side])
        def _():
            for copy in halo_copies(side):
                copy.start()

    rest = img.at[:, pl.ds(0, (n - 1) * Y)]
    pltpu.make_async_copy(rest, rest, img_sem.at[1]).wait()

    def laplace():
        ld_local.wait()
        halo_wait(halo_recv)
        for side in "lr":
            @pl.when(has[side])
            def _():
                wext[edge[side][0], edge[side][1], :] = decode(edge_in, edge_scale_in, num[side])

        wide = lax.broadcasted_iota(jnp.int32, (Z, X), 1)

        def plane(y, carry):
            centre = wext[y + R, pl.ds(8, Z), :]
            running = 3.0 * STENCIL[0] * centre
            for r in range(1, R + 1):
                beside = wext[y + R + r, pl.ds(8, Z), :] + wext[y + R - r, pl.ds(8, Z), :]
                beside = beside + wext[y + R, pl.ds(8 + r, Z), :]
                beside = beside + wext[y + R, pl.ds(8 - r, Z), :]
                beside = beside + jnp.where(wide < X - r, pltpu.roll(centre, X - r, 1), 0.0)
                beside = beside + jnp.where(wide >= r, pltpu.roll(centre, r, 1), 0.0)
                running = running + STENCIL[r] * beside
            fin[y] = 2.0 * centre - prev[y] + cour[y] * (running + acc[y])
            return carry

        lax.fori_loop(0, Y, plane, 0)

    early = jnp.logical_and(jnp.logical_and(me >= 2, me < n - 1), shot == 0)

    @pl.loop(0, (n - 1) * pieces)
    def _(q):
        swap = jnp.where(q == 0, pieces, jnp.where(q <= pieces, q - 1, q))
        turns = q
        if pieces == 2 and n > 2:
            turns = jnp.where(shot == 0, jnp.where(q < 2, q + 2, jnp.where(q < 4, q - 2, q)), jnp.where(q == 1, 2, jnp.where(q == 2, 1, q)))
        q = jnp.where(early, swap, jnp.where(me == 1, turns, q))
        i, c = q // pieces, q % pieces
        j = order(i)

        @pl.when(jnp.logical_and(me == 0, q == (n - 2) * pieces))
        def _():
            laplace()

        onward, go_on = relay(j)
        bg_copy(j, c, far(j), place(j, me), bg_send.at[0]).wait_recv()

        @pl.when(go_on)
        def _():
            bg_copy(j, c, {"off": onward}, place(j, onward), bg_send.at[0]).start()

        @pl.when(jnp.logical_and(c == 0, jnp.logical_and(j > me, relayed(me, j, shot))))
        def _():
            pl.semaphore_wait(ready.at[j - 1], 1)
        total = partial(j, c)
        later = jnp.logical_and(joins, j == me + 1)

        @pl.when(later)
        def _():
            pend[pl.ds(c * step, step)] = total

        @pl.when(jnp.logical_not(later))
        def _():
            encode(total, part_out, scale_out, j, c)
            part_send(j, c)

    @pl.when(joins)
    def _():
        for c in range(pieces):
            pltpu.make_async_copy(piece_tally, piece_tally, join_recv.at[c]).wait()
            total = pend[pl.ds(c * step, step)] + decode(join_in, join_scale, c)
            encode(total, part_out, scale_out, me + 1, c)
            part_send(me + 1, c)

    @pl.when(me > 0)
    def _():
        laplace()

    def drain():
        halo_wait(halo_send)
        sent, passed = 0, 0
        for g in range(n):
          there = g != me
          sent = sent + jnp.logical_and(there, direct(g)).astype(jnp.int32)
          passed = passed + jnp.logical_and(there, relay(g)[1]).astype(jnp.int32)
        bg_sent(bg_send.at[0], sent + passed, 2 * n)
        pltpu.make_async_copy(tally, tally, p_send.at[0]).wait()

    @pl.loop(0, n - 1)
    def _(i):
        j = order(i)

        @pl.when(i == n - 2)
        def _():
            drain()

        @pl.when(j != me - 2)
        def _():
            pltpu.make_async_copy(tally.at[0], tally.at[0], p_recv.at[place(j, me)]).wait()
            for c in range(pieces):
                rows = pl.ds(c * step, step)
                fin[rows] = fin[rows] + cour[rows] * decode(part_in, scale_in, j, c)


def on_device(n, nd, image, offset_of, background, wave_now, wave_prev, courant):
    K, rows, Z, X = image.shape
    Y = wave_now.shape[1]
    f32 = jnp.float32
    pieces = PIECES if Y % PIECES == 0 else 1
    step = Y // pieces
    lines = (Y * Z * X * 2) // (LANES * 4) + pieces
    dma = pltpu.SemaphoreType.DMA
    regular = pltpu.SemaphoreType.REGULAR
    return pl.pallas_call(
        functools.partial(kernel, n, nd),
        out_shape=jax.ShapeDtypeStruct(wave_now.shape, f32),
        in_specs=[pl.BlockSpec(memory_space=pltpu.HBM)] * 6,
        out_specs=pl.BlockSpec(memory_space=pltpu.VMEM),
        scratch_shapes=[
            pltpu.SMEM((K,), jnp.int32),
            pltpu.VMEM((K, rows, Z, X), jnp.bfloat16),
            pltpu.VMEM((Y, Z, X), jnp.bfloat16),
            pltpu.VMEM((n, Y, Z, X), jnp.bfloat16),
            pltpu.VMEM((Y + 2 * R, Z + 16, X), f32),
            pltpu.VMEM((2, Y, Z, X), f32),
            pltpu.VMEM(((K + 1) // 2, 2 * LANES, 2 * LANES), jnp.bfloat16),
            pltpu.VMEM((Y, Z, X), f32),
            pltpu.VMEM((n, pieces, step, Z, X), jnp.int16),
            pltpu.VMEM((n, pieces, step, Z, X), jnp.int16),
            pltpu.VMEM((n, pieces, 1, LANES), f32),
            pltpu.VMEM((n, pieces, 1, LANES), f32),
            pltpu.VMEM((Y, Z, X), f32),
            pltpu.VMEM((pieces, step, Z, X), jnp.int16),
            pltpu.VMEM((pieces, 1, LANES), f32),
            pltpu.VMEM((n - 1, lines, LANES), f32),
            pltpu.VMEM((2, R, Z, X), jnp.int16),
            pltpu.VMEM((2, R, Z, X), jnp.int16),
            pltpu.VMEM((2, 1, LANES), f32),
            pltpu.VMEM((2, 1, LANES), f32),
            pltpu.VMEM((2, (R * Z * X * 2) // (LANES * 4) + 1, LANES), f32),
            pltpu.VMEM((lines // pieces, LANES), f32),
            dma((4,)), dma((2,)), regular((n - 1,)), regular((1,)),
            dma(((n - 1) * pieces,)), dma((1,)), dma((2,)), dma((2,)),
            dma((n - 1,)), dma((pieces,)), dma((1,)),
        ],
        compiler_params=pltpu.CompilerParams(
            collective_id=0, has_side_effects=True, vmem_limit_bytes=50331648),
        name="born_step",
    )(*[pltpu.with_memory_space_constraint(a, pltpu.HBM) for a in
        (offset_of, image, background, wave_now, wave_prev, courant)])


def solution(mesh):
    wave = P(("parts", "shot"), "off", "depth", None)
    return jax.shard_map(
        functools.partial(on_device, mesh.shape["off"], mesh.shape["depth"]),
        mesh=mesh,
        in_specs=(
            P("off", None, "depth", None),
            P("off"),
            wave,
            wave,
            wave,
            P("off", "depth", None),
        ),
        out_specs=wave,
        check_vma=False,
    )
```
